128 devices in a mesh: tx: 8 (over y, core), ty: 16 (over z, x).
Axes of the slice: x: 4, y: 4, z: 4, core: 2. Of those that a mesh axis runs over, the one named last changes fastest.
Arguments:
- increments: bfloat16 [3, 8, 1152, 4096], P(None, None, 'tx', 'ty'), may hold values from -6 to 6
- remap_weights: bfloat16 [8, 16, 144, 2, 128, 256], P('tx', 'ty'), may hold values from -0.375 to 0.375
- dest_offset: int32 [8, 16, 144, 2], P('tx', 'ty'), may hold values from 0 to 3, as said below
- slot_patch: int32 [8, 16, 4, 108], P('tx', 'ty'), may hold values from 0 to 143, as said below
- rotation: int32 [2, 4], replicated, may hold values from 0 to 3
- basis: float32 [4, 768, 3072], P(None, 'ty', 'tx'), may hold values from -4 to 4
- inv_metric_diag: float32 [2, 768, 3072], P(None, 'ty', 'tx'), may hold values from 0.7 to 1.7
- inv_metric_cross: float32 [768, 3072], P('ty', 'tx'), may hold values from -0.5 to 0.5
- thickness: float32 [8, 768, 3072], P(None, 'ty', 'tx'), may hold values from -6 to 6
- wind_first: float32 [8, 768, 3072], P(None, 'ty', 'tx'), may hold values from -6 to 6
- wind_second: float32 [8, 768, 3072], P(None, 'ty', 'tx'), may hold values from -6 to 6
Outputs:
- thickness_new: float32 [8, 768, 3072], P(None, 'ty', 'tx')
- wind_first_new: float32 [8, 768, 3072], P(None, 'ty', 'tx')
- wind_second_new: float32 [8, 768, 3072], P(None, 'ty', 'tx')
The draws below stay inside these ranges and needn't reach their ends.
Inputs may be any that keep to these rules, and one draw needn't show every extreme that they name: `dest_offset`: the intersections of one block name every one of the 4 distances at least 36 and at most 108 times, and one of them exactly 108 times. In every tx row some tile owner receives exactly 108 intersections from each of the 4 blocks that send to it. `slot_patch`: slots past the number of intersections that arrive from a sender receive nothing. The used slots of one tile owner name every one of its 144 patches at least once.
All inputs are finite; a program needn't handle non-finite values.
Results may differ from the reference program's by a relative error of at most 0.0003.
Values sent between devices are 32-bit elements; how exact they have to be, the bound alone decides.
A program may use at most 192 MiB of HBM per device.

```python
import jax
import jax.numpy as jnp
from jax import lax

L = 8
PANELS = 4
STEPS = 4
TC = 384
TR = 48
TPATCH = 128
SC = 256
TOP = 2
OWNERS = 4
TP = 144
SR = 144
LO = 36
CAP = 108
NR = 768
NC = 3072
LATS = 1152
LONS = 4096
N_TX = 8
N_TY = 16


def intersection_plan(key):
    base_key = jax.random.fold_in(key, 11)
    subkeys = jax.random.split(base_key, 6)
    offsets = jnp.arange(OWNERS, dtype=jnp.int32)
    heavy_offset = jax.random.randint(subkeys[0], (N_TX, N_TY), 0, OWNERS)
    chosen = jax.random.randint(subkeys[1], (N_TX, 1), 0, N_TY)
    columns = jnp.arange(N_TY, dtype=jnp.int32)[None, :]
    forced = (chosen - columns) % N_TY
    heavy_offset = jnp.where(forced < OWNERS, forced, heavy_offset)
    pick_ids = jax.random.randint(subkeys[2], (N_TX, N_TY, 2 * LO), 0, OWNERS - 1)
    pick_ids = pick_ids + (pick_ids >= heavy_offset[:, :, None]).astype(jnp.int32)
    extra_count = jnp.sum((pick_ids[:, :, :, None] == offsets[None, None, None, :]).astype(jnp.int32), axis=2)
    counts = jnp.where(offsets[None, None, :] == heavy_offset[:, :, None], CAP, LO + extra_count).astype(jnp.int32)
    return (counts, subkeys)


def draw_dest_offset(key, part):
    counts, subkeys = intersection_plan(key)
    entries = SR * TOP
    bounds = jnp.cumsum(counts, axis=2).astype(jnp.int32)
    entry_ids = jnp.arange(entries, dtype=jnp.int32)
    ordered = jnp.sum((entry_ids[None, None, :, None] >= bounds[:, :, None, :OWNERS - 1]).astype(jnp.int32), axis=3)
    shuffles = jax.vmap(lambda one_key: jax.random.permutation(one_key, entries))(jax.random.split(subkeys[3], N_TX * N_TY))
    shuffles = shuffles.reshape(N_TX, N_TY, entries).astype(jnp.int32)
    return jnp.take_along_axis(ordered, shuffles, axis=2).reshape(N_TX, N_TY, SR, TOP).astype(jnp.int32)


def draw_slot_patch(key, part):
    counts, subkeys = intersection_plan(key)
    offsets = jnp.arange(OWNERS, dtype=jnp.int32)
    sources = (jnp.arange(N_TY, dtype=jnp.int32)[:, None] - offsets[None, :]) % N_TY
    arriving = counts[:, sources, offsets[None, :]]
    starts = (jnp.cumsum(arriving, axis=2) - arriving).astype(jnp.int32)
    slots = jnp.arange(CAP, dtype=jnp.int32)
    running = starts[:, :, :, None] + slots[None, None, None, :]
    shuffles = jax.vmap(lambda one_key: jax.random.permutation(one_key, TP))(jax.random.split(subkeys[4], N_TX * N_TY))
    shuffles = shuffles.reshape(N_TX, N_TY, TP).astype(jnp.int32)
    used = jnp.take_along_axis(shuffles, (running % TP).reshape(N_TX, N_TY, OWNERS * CAP), axis=2).reshape(N_TX, N_TY, OWNERS, CAP)
    filler = jax.random.randint(subkeys[5], (N_TX, N_TY, OWNERS, CAP), 0, TP)
    return jnp.where(slots[None, None, None, :] < arriving[:, :, :, None], used, filler).astype(jnp.int32)


def set_ends(values, stream_key, least, largest):
    index_at = [jax.random.randint(jax.random.fold_in(stream_key, axis), (), 0, length) for axis, length in enumerate(values.shape)]
    main_axis = values.shape.index(max(values.shape))
    next_to = index_at[:main_axis] + [(index_at[main_axis] + 1) % values.shape[main_axis]] + index_at[main_axis + 1:]
    return values.at[tuple(index_at)].set(least).at[tuple(next_to)].set(largest)


def steps_of(key, shape, cuts, smallest, top_value):
    def one(dim, shards_of):
        heights = jax.random.uniform(jax.random.fold_in(jax.random.fold_in(key, 6), dim), (shards_of,), jnp.float32, smallest / len(cuts), top_value / len(cuts))
        return jnp.repeat(jnp.exp(heights), shape[dim] // shards_of).reshape((-1,) + (1,) * (len(shape) - dim - 1))

    gain = one(*cuts[0])
    for cut in cuts[1:]:
        gain = gain * one(*cut)
    return gain


def gaussian(key, shape, width, reach, shards=(), kind=jnp.bfloat16):
    result = jax.random.normal(key, shape, jnp.float32) * width
    if len(shards) > 0:
        result = steps_of(key, shape, shards, -0.22, 0.18) * result
    return jnp.clip(result, min=-reach, max=reach).astype(kind)


def setup_inputs(seed: int = 0) -> dict:
    seeds = jax.random.split(jax.random.key(seed), 12)
    return {
        "increments": gaussian(seeds[0], (3, L, LATS, LONS), 1.0, 6.0, ((2, 8), (3, 16))),
        "remap_weights": gaussian(seeds[1], (N_TX, N_TY, SR, TOP, TPATCH, SC), SC ** -0.5, 0.375, ((0, 8), (1, 16))),
        "dest_offset": draw_dest_offset(jax.random.fold_in(seeds[11], 71), 0),
        "slot_patch": draw_slot_patch(jax.random.fold_in(seeds[11], 71), 0),
        "rotation": set_ends(jax.random.randint(seeds[4], (2, PANELS), 0, 4), jax.random.fold_in(seeds[4], 1), 0, 3).astype(jnp.int32),
        "basis": gaussian(seeds[5], (4, NR, NC), 1.0, 4.0, ((1, 16), (2, 8)), jnp.float32),
        "inv_metric_diag": jnp.clip(0.7 + 1 * jax.random.uniform(seeds[6], (2, NR, NC), jnp.float32) ** steps_of(seeds[6], (2, NR, NC), ((1, 16), (2, 8)), -0.2, 0.2), 0.7, 1.7),
        "inv_metric_cross": jnp.clip(jax.random.uniform(seeds[7], (NR, NC), jnp.float32, -0.5, 0.5) * steps_of(seeds[7], (NR, NC), ((0, 16), (1, 8)), -0.4, 0.0), -0.5, 0.5),
        "thickness": gaussian(seeds[8], (L, NR, NC), 1.0, 6.0, ((1, 16), (2, 8)), jnp.float32),
        "wind_first": gaussian(seeds[9], (L, NR, NC), 1.0, 6.0, ((1, 16), (2, 8)), jnp.float32),
        "wind_second": gaussian(seeds[10], (L, NR, NC), 1.0, 6.0, ((1, 16), (2, 8)), jnp.float32),
    }


COURANT = 0.15
GRADIENT = 0.3


def quarter_turn(code):
    cosine = (code == 0).astype(jnp.float32) - (code == 2).astype(jnp.float32)
    sine_value = (code == 1).astype(jnp.float32) - (code == 3).astype(jnp.float32)
    return cosine, sine_value


def advance(depth, cov_first, cov_second, con_first, con_second, depth_below, second_below, depth_above, second_above, depth_left, first_left, depth_right, first_right, wall_left, wall_right):
    face_below = 0.5 * (con_second + second_below)
    flux_below = jnp.maximum(face_below, 0.0) * depth_below + jnp.minimum(face_below, 0.0) * depth
    face_above = 0.5 * (con_second + second_above)
    flux_above = jnp.maximum(face_above, 0.0) * depth + jnp.minimum(face_above, 0.0) * depth_above
    face_left = 0.5 * (con_first + first_left) * wall_left
    flux_left = jnp.maximum(face_left, 0.0) * depth_left + jnp.minimum(face_left, 0.0) * depth
    face_right = 0.5 * (con_first + first_right) * wall_right
    flux_right = jnp.maximum(face_right, 0.0) * depth + jnp.minimum(face_right, 0.0) * depth_right
    new_depth = depth - COURANT * ((flux_right - flux_left) + (flux_above - flux_below))
    new_first = cov_first - GRADIENT * 0.5 * (depth_right - depth_left)
    new_second = cov_second - GRADIENT * 0.5 * (depth_above - depth_below)
    return new_depth, new_first, new_second


def reference(increments, remap_weights, dest_offset, slot_patch, rotation, basis, inv_metric_diag, inv_metric_cross, thickness, wind_first, wind_second):
    row_width = 3 * L * TPATCH
    entries = SR * TOP
    block_count = N_TX * N_TY
    blocks = increments.reshape(3, L, N_TX, SR, N_TY, SC).transpose(2, 4, 0, 1, 3, 5).reshape(block_count, 3, L, SR, SC)
    weights = remap_weights.reshape(block_count, SR, TOP, TPATCH, SC)

    def one_block(pair):
        block, weight = pair
        partial_terms = jnp.einsum("clsk,stpk->stclp", block.astype(jnp.float32), weight.astype(jnp.float32))
        return partial_terms.reshape(entries, row_width)

    contrib = lax.map(one_block, (blocks, weights))
    block_ids = jnp.arange(block_count, dtype=jnp.int32)
    tile_row = block_ids // N_TY
    tile_col = block_ids % N_TY
    offsets = dest_offset.reshape(block_count, entries).astype(jnp.int32)
    onehot = (offsets[:, :, None] == jnp.arange(OWNERS, dtype=jnp.int32)[None, None, :]).astype(jnp.int32)
    earlier = (jnp.cumsum(onehot, axis=1) - onehot).astype(jnp.int32)
    slot_index = jnp.sum(earlier * onehot, axis=2).astype(jnp.int32)
    receiver = ((tile_col[:, None] + offsets) % N_TY).astype(jnp.int32)
    patch_id = slot_patch[tile_row[:, None], receiver, offsets, slot_index].astype(jnp.int32)
    target = ((tile_row[:, None] * N_TY + receiver) * TP + patch_id).reshape(-1).astype(jnp.int32)
    patches = jnp.zeros((block_count * TP, row_width), jnp.float32).at[target].add(contrib.reshape(-1, row_width))
    blocks_per_row = TC // TPATCH
    tiles = patches.reshape(N_TX, N_TY, TR, blocks_per_row, 3, L, TPATCH).transpose(4, 5, 1, 2, 0, 3, 6).reshape(3, L, NR, NC)
    cov_first = wind_first + basis[0] * tiles[0] + basis[1] * tiles[1]
    cov_second = wind_second + basis[2] * tiles[0] + basis[3] * tiles[1]
    depth = thickness + tiles[2]

    rows_all = jnp.arange(NR, dtype=jnp.int32)
    panel_rows = NR // PANELS
    panel = rows_all // panel_rows
    code_below = jnp.where(rows_all % panel_rows == 0, rotation[0][panel], 0)
    code_above = jnp.where(rows_all % panel_rows == panel_rows - 1, rotation[1][panel], 0)
    cos_below, sin_below = quarter_turn(code_below[:, None])
    cos_above, sin_above = quarter_turn(code_above[:, None])
    columns = jnp.arange(NC, dtype=jnp.int32)
    wall_left = jnp.where(columns == 0, 0.0, 1.0).astype(jnp.float32)
    wall_right = jnp.where(columns == NC - 1, 0.0, 1.0).astype(jnp.float32)
    zero_column = jnp.zeros((L, NR, 1), jnp.float32)

    for iteration in range(STEPS):
        con_first = inv_metric_diag[0] * cov_first + inv_metric_cross * cov_second
        con_second = inv_metric_cross * cov_first + inv_metric_diag[1] * cov_second
        depth_below = jnp.roll(depth, 1, axis=1)
        second_below = sin_below * jnp.roll(con_first, 1, axis=1) + cos_below * jnp.roll(con_second, 1, axis=1)
        depth_above = jnp.roll(depth, -1, axis=1)
        second_above = sin_above * jnp.roll(con_first, -1, axis=1) + cos_above * jnp.roll(con_second, -1, axis=1)
        depth_left = jnp.concatenate([zero_column, depth[:, :, :-1]], axis=2)
        first_left = jnp.concatenate([zero_column, con_first[:, :, :-1]], axis=2)
        depth_right = jnp.concatenate([depth[:, :, 1:], zero_column], axis=2)
        first_right = jnp.concatenate([con_first[:, :, 1:], zero_column], axis=2)
        depth, cov_first, cov_second = advance(depth, cov_first, cov_second, con_first, con_second, depth_below, second_below, depth_above, second_above, depth_left, first_left, depth_right, first_right, wall_left, wall_right)
    return depth, cov_first, cov_second
```

```python
import jax
import jax.numpy as jnp
from jax import lax
from jax.experimental import pallas as pl
from jax.experimental.pallas import tpu as pltpu
from jax.sharding import PartitionSpec as P

MESH = pl.DeviceIdType.MESH
PANELS = 4
STEPS = 4
HALO = 4
COURANT = 0.15
HALF_GRADIENT = 0.15
LANES = 128
GROUPS = 32
NX = 4
SEND_CHUNKS = 6
W_SLOTS = 4
W_ROWS = 16


def kernel(
    perm, prev, last, turn, inc, wts, basis, diag, cross, depth_in, first_in, second_in,
    out_depth, out_first, out_second,
    wbuf, inc_v, half0, half1, term, send, recv, relay, acc, xa, xb, metric, bases,
    state_in, out_v, grid_raw, grid_side, basis_raw, packed, strips,
    w_sem, in_sem, field_sem, out_sem, send_sem, recv_sem, relay_send_sem, relay_recv_sem,
    grid_send_sem, grid_recv_sem, halo_send_sem, halo_recv_sem,
):
    tx = lax.axis_index("tx")
    ty = lax.axis_index("ty")
    n_tx = lax.axis_size("tx")
    n_ty = lax.axis_size("ty")
    x = lax.rem(ty, NX)
    odd = lax.rem(tx, 2) == 1
    flows, capacity = send.shape[0], send.shape[1]
    entries = term.shape[0] - 1
    slots = acc.shape[0] - 1
    per = capacity // SEND_CHUNKS
    rows = state_in.shape[3]
    levels = state_in.shape[2]
    blocks = state_in.shape[1]
    w_chunks = wts.shape[0] // W_ROWS

    def dev(dx, dy):
        return (lax.rem(tx + dx + n_tx, n_tx), lax.rem(ty + dy + n_ty, n_ty))

    barrier = pltpu.get_barrier_semaphore()
    partners = [(0, s * d) for d in (1, 2, 3, 4) for s in (1, -1)]
    partners += [(s, d) for s in (1, -1) for d in (-1, 0, 1)]
    for dx, dy in partners:
        pl.semaphore_signal(barrier, inc=1, device_id=dev(dx, dy), device_id_type=MESH)

    def w_copy(chunk, slot):
        return pltpu.make_async_copy(wts.at[pl.ds(chunk * W_ROWS, W_ROWS)], wbuf.at[slot], w_sem.at[slot])

    inc_copy = pltpu.make_async_copy(inc, inc_v, in_sem)
    inc_copy.start()
    for slot in range(W_SLOTS):
        w_copy(slot, slot).start()
    field_copies = [
        pltpu.make_async_copy(diag, grid_raw.at[0:2, 8 : 8 + rows], field_sem.at[0]),
        pltpu.make_async_copy(cross, grid_raw.at[2, 8 : 8 + rows], field_sem.at[1]),
        pltpu.make_async_copy(basis, basis_raw, field_sem.at[2]),
    ]
    for i, field in enumerate((depth_in, first_in, second_in)):
        for b in range(blocks):
            field_copies.append(
                pltpu.make_async_copy(
                    field.at[:, :, b * LANES : (b + 1) * LANES], state_in.at[i, b], field_sem.at[3 + i * blocks + b]
                )
            )
    for copy in field_copies:
        copy.start()

    zero_row = jnp.zeros(term.shape[1:], jnp.float32)
    term[entries] = zero_row
    acc[slots] = zero_row

    inc_copy.wait()

    def term_chunk(chunk, carry):
        slot = lax.rem(chunk, W_SLOTS)
        start = pl.multiple_of(chunk * W_ROWS, W_ROWS)
        cells = inc_v[:, pl.ds(start, W_ROWS), :].astype(jnp.float32)
        pairs = cells.shape[0]
        half0[...] = cells[:, :, :LANES].reshape(pairs * W_ROWS, LANES)
        half1[...] = cells[:, :, LANES:].reshape(pairs * W_ROWS, LANES)
        w_copy(chunk, slot).wait()
        for s in range(W_ROWS):
            lhs = jnp.concatenate(
                [half0[pl.ds(s, pairs, stride=W_ROWS), :], half1[pl.ds(s, pairs, stride=W_ROWS), :]], axis=1
            ).astype(jnp.bfloat16)
            product = lax.dot_general(
                lhs, wbuf[slot, s], (((1,), (1,)), ((), ())), preferred_element_type=jnp.float32
            )
            entry = 2 * (start + s)
            term[entry] = product[:, :LANES]
            term[entry + 1] = product[:, LANES:]

        @pl.when(chunk + W_SLOTS < w_chunks)
        def _():
            w_copy(chunk + W_SLOTS, slot).start()

        return carry

    lax.fori_loop(0, w_chunks, term_chunk, 0)

    pl.semaphore_wait(barrier, len(partners))

    def direct(d, c):
        part = pl.ds(c * per, per)
        return pltpu.make_async_remote_copy(
            send.at[d - 1, part], recv.at[d - 1, part], send_sem.at[d - 1, c], recv_sem.at[d - 1, c],
            device_id=dev(0, d), device_id_type=MESH,
        )

    def first_leg(d, c):
        part = pl.ds(c * per, per)
        return pltpu.make_async_remote_copy(
            send.at[d - 1, part], relay.at[d - 1, part], send_sem.at[d - 1, c], relay_recv_sem.at[d - 1, c],
            device_id=dev(0, NX), device_id_type=MESH,
        )

    def second_leg(d, c):
        part = pl.ds(c * per, per)
        return pltpu.make_async_remote_copy(
            relay.at[d - 1, part], recv.at[d - 1, part], relay_send_sem.at[d - 1, c], recv_sem.at[d - 1, c],
            device_id=dev(0, d - NX), device_id_type=MESH,
        )

    def relayed(d):
        return jnp.logical_and(odd, x + d >= NX)

    def send_chunk(c, carry):
        for d in range(1, flows + 1):

            def gather(i, inner):
                k = c * per + i
                send[d - 1, k] = term[perm[d * capacity + k]]
                return inner

            lax.fori_loop(0, per, gather, 0, unroll=6)

            @pl.when(relayed(d))
            def _():
                first_leg(d, c).start()

            @pl.when(jnp.logical_not(relayed(d)))
            def _():
                direct(d, c).start()

        return carry

    lax.fori_loop(0, SEND_CHUNKS, send_chunk, 0)

    for copy in field_copies:
        copy.wait()

    own = slice(8, 8 + rows)
    low = slice(8, 16)
    high = slice(rows, 8 + rows)
    below = slice(0, 8)
    above = slice(8 + rows, 16 + rows)
    left = slice(0, LANES)
    right = slice((blocks - 1) * LANES, blocks * LANES)
    grid_moves = [
        (grid_raw.at[:, low], grid_raw.at[:, above], (0, -1)),
        (grid_raw.at[:, high], grid_raw.at[:, below], (0, 1)),
        (grid_raw.at[:, own, left], grid_side.at[0, :, own], (-1, 0)),
        (grid_raw.at[:, low, left], grid_side.at[0, :, above], (-1, -1)),
        (grid_raw.at[:, high, left], grid_side.at[0, :, below], (-1, 1)),
        (grid_raw.at[:, own, right], grid_side.at[1, :, own], (1, 0)),
        (grid_raw.at[:, low, right], grid_side.at[1, :, above], (1, -1)),
        (grid_raw.at[:, high, right], grid_side.at[1, :, below], (1, 1)),
    ]
    grid_copies = [
        pltpu.make_async_remote_copy(
            src, dst, grid_send_sem.at[i], grid_recv_sem.at[i], device_id=dev(*to), device_id_type=MESH
        )
        for i, (src, dst, to) in enumerate(grid_moves)
    ]
    for copy in grid_copies:
        copy.start()

    def accumulate_own(i, carry):
        acc[i] = term[perm[i]] + acc[prev[i]]
        return carry

    lax.fori_loop(0, capacity, accumulate_own, 0, unroll=4)

    shape = (levels, LANES)
    lane = lax.broadcasted_iota(jnp.int32, shape, 1)
    keep_right = jnp.where(tx < n_tx - 1, 1.0, 0.0).astype(jnp.float32)
    keep_left = jnp.where(tx > 0, 1.0, 0.0).astype(jnp.float32)

    def spread(block, j):
        return jnp.broadcast_to(block[j : j + 1], shape)

    def spread_basis(t, carry):
        at = pl.ds(pl.multiple_of(t * 8, 8), 8)
        for k in range(4):
            for b in range(blocks):
                block = basis_raw[k, at, b * LANES : (b + 1) * LANES]
                for j in range(8):
                    bases[k, t * 8 + j, b] = spread(block, j)
        return carry

    lax.fori_loop(0, rows // 8, spread_basis, 0)

    for copy in grid_copies:
        copy.wait_recv()

    def spread_metric(t, carry, picks=range(8)):
        at = pl.ds(pl.multiple_of(t * 8, 8), 8)
        base = t * 8 - 8 + HALO
        for k in range(3):
            for b in range(blocks):
                block = grid_raw[k, at, b * LANES : (b + 1) * LANES]
                for j in picks:
                    metric[k, base + j, b] = spread(block, j)
            side = jnp.where(lane < LANES // 2, grid_side[0, k, at, :] * keep_right, grid_side[1, k, at, :] * keep_left)
            for j in picks:
                metric[k, base + j, blocks] = spread(side, j)
        return carry

    spread_metric(0, 0, range(8 - HALO, 8))
    lax.fori_loop(1, 1 + rows // 8, spread_metric, 0)
    spread_metric(1 + rows // 8, 0, range(HALO))

    def receive_chunk(c, carry):
        for d in range(1, flows + 1):

            @pl.when(relayed(d))
            def _():
                first_leg(d, c).wait_recv()
                second_leg(d, c).start()

        for d in range(1, flows + 1):
            direct(d, c).wait_recv()
            base = capacity + (c * flows + d - 1) * per

            def add(i, inner):
                acc[base + i] = recv[d - 1, c * per + i] + acc[prev[base + i]]
                return inner

            lax.fori_loop(0, per, add, 0, unroll=6)
        return carry

    lax.fori_loop(0, SEND_CHUNKS, receive_chunk, 0)

    def regrid(r, carry):
        for b in range(blocks):
            patch = acc.at[last[r * blocks + b]]
            east, north, thick = patch[0:levels], patch[levels : 2 * levels], patch[2 * levels : 3 * levels]
            at = pl.ds(r, levels, stride=rows)

            def start(i):
                return state_in.at[i, b].reshape(levels * rows, LANES)[at, :]

            xa[0, r + HALO, b] = start(0) + thick
            xa[1, r + HALO, b] = start(1) + bases[0, r, b] * east + bases[1, r, b] * north
            xa[2, r + HALO, b] = start(2) + bases[2, r, b] * east + bases[3, r, b] * north
        return carry

    lax.fori_loop(0, HALO, regrid, 0)
    lax.fori_loop(rows - HALO, rows, regrid, 0)

    def halo_copy(i, src, dst, to):
        return pltpu.make_async_remote_copy(
            src, dst, halo_send_sem.at[i], halo_recv_sem.at[i], device_id=dev(*to), device_id_type=MESH
        )

    row_copies = [
        halo_copy(0, xa.at[:, HALO : 2 * HALO, 0:blocks], xa.at[:, rows + HALO : rows + 2 * HALO, 0:blocks], (0, -1)),
        halo_copy(1, xa.at[:, rows : rows + HALO, 0:blocks], xa.at[:, 0:HALO, 0:blocks], (0, 1)),
    ]
    for copy in row_copies:
        copy.start()

    lax.fori_loop(HALO, rows - HALO, regrid, 0)

    group = lane // HALO
    packs = packed.shape[1]
    for side in range(2):
        for v in range(packs):
            total = jnp.zeros(shape, jnp.float32)
            for g in range(GROUPS):
                item = v * GROUPS + g
                if item >= 3 * rows:
                    break
                edge = xa[item % 3, item // 3 + HALO, 0 if side == 0 else blocks - 1]
                shift = (HALO * g + (HALO if side else 0)) % LANES
                moved = pltpu.roll(edge, shift, 1) if shift else edge
                total = jnp.where(group == g, moved, total)
            packed[side, v] = total

    strip_copies = []
    for side, dx in ((0, -1), (1, 1)):
        strip_copies += [
            halo_copy(2 + 3 * side, packed.at[side], strips.at[side, 0:packs], (dx, 0)),
            halo_copy(3 + 3 * side, packed.at[side, 0:1], strips.at[side, packs + 1 : packs + 2], (dx, -1)),
            halo_copy(4 + 3 * side, packed.at[side, packs - 1 : packs], strips.at[side, packs : packs + 1], (dx, 1)),
        ]
    for copy in strip_copies:
        copy.start()
    for copy in strip_copies:
        copy.wait_recv()

    for r in range(-HALO, rows + HALO):
        for f in range(3):
            item = 3 * (r % rows) + f
            g = item % GROUPS
            v = item // GROUPS
            if r < 0:
                v = packs
            elif r >= rows:
                v = packs + 1
            from_right = pltpu.roll(strips[0, v], (LANES - HALO * g) % LANES, 1) if g else strips[0, v]
            from_left = pltpu.roll(strips[1, v], (LANES - HALO - HALO * g) % LANES, 1) if g < GROUPS - 1 else strips[1, v]
            xa[f, r + HALO, blocks] = jnp.where(
                lane < HALO,
                from_right * keep_right,
                jnp.where(lane >= LANES - HALO, from_left * keep_left, 0.0),
            )
    for copy in row_copies:
        copy.wait_recv()

    ring = blocks + 1
    is_first = lane == 0
    is_last = lane == LANES - 1
    one = jnp.ones(shape, jnp.float32)
    wall_right = jnp.where(is_last, keep_right, one)
    wall_left = jnp.where(is_last, keep_left, one)

    def from_next(values):
        rolled = [pltpu.roll(v, LANES - 1, 1) for v in values]
        return [jnp.where(is_last, rolled[(b + 1) % ring], rolled[b]) for b in range(ring)]

    def from_before(values):
        rolled = [pltpu.roll(v, 1, 1) for v in values]
        return [jnp.where(is_first, rolled[(b - 1) % ring], rolled[b]) for b in range(ring)]

    def load(src, i):
        depth, con_first, con_second = [], [], []
        for b in range(ring):
            first, second = src[1, i, b], src[2, i, b]
            depth.append(src[0, i, b])
            con_first.append(metric[0, i, b] * first + metric[2, i, b] * second)
            con_second.append(metric[2, i, b] * first + metric[1, i, b] * second)
        return depth, con_first, con_second

    def row_flux(second_low, second_high, depth_low, depth_high):
        out = []
        for b in range(ring):
            face = 0.5 * (second_low[b] + second_high[b])
            out.append(jnp.maximum(face, 0.0) * depth_low[b] + jnp.minimum(face, 0.0) * depth_high[b])
        return out

    def turned(joint, con_first, con_second):
        return [turn[2 * joint] * con_first[b] + turn[2 * joint + 1] * con_second[b] for b in range(ring)]

    def advance_row(src, store, i, carry, joint=None):
        depth_before, (depth, con_first, con_second), flux_below = carry
        after = load(src, i + 1)
        depth_after, first_after, second_after = after
        if joint is None:
            flux_above = row_flux(con_second, second_after, depth, depth_after)
            flux_next = flux_above
        else:
            flux_above = row_flux(con_second, turned(joint, first_after, second_after), depth, depth_after)
            flux_next = row_flux(turned(joint + 1, con_first, con_second), second_after, depth, depth_after)
        depth_right = from_next(depth)
        first_right = from_next(con_first)
        flux_right = []
        for b in range(ring):
            face = 0.5 * (con_first[b] + first_right[b])
            if b == blocks - 1:
                face = face * wall_right
            if b == blocks:
                face = face * wall_left
            flux_right.append(jnp.maximum(face, 0.0) * depth[b] + jnp.minimum(face, 0.0) * depth_right[b])
        depth_left = from_before(depth)
        flux_left = from_before(flux_right)
        for b in range(ring):
            new_depth = depth[b] - COURANT * ((flux_right[b] - flux_left[b]) + (flux_above[b] - flux_below[b]))
            new_first = src[1, i, b] - HALF_GRADIENT * (depth_right[b] - depth_left[b])
            new_second = src[2, i, b] - HALF_GRADIENT * (depth_after[b] - depth_before[b])
            store(i, b, (new_depth, new_first, new_second))
        return (depth, after, flux_next)

    for step in range(STEPS):
        src, dst = (xa, xb) if step % 2 == 0 else (xb, xa)
        margin = STEPS - 1 - step

        def store_state(i, b, values, dst=dst):
            for f in range(3):
                dst[f, i, b] = values[f]

        def store_out(i, b, values):
            if b < blocks:
                for f in range(3):
                    out_v.at[f, b].reshape(levels * rows, LANES)[pl.ds(i - HALO, levels, stride=rows), :] = values[f]

        if step == 1:
            for copy in row_copies:
                copy.wait_send()
        store = store_out if step == STEPS - 1 else store_state
        start = HALO - margin
        before, current = load(src, start - 1), load(src, start)
        if margin == 0:
            flux = row_flux(turned(1, before[1], before[2]), current[2], before[0], current[0])
        else:
            flux = row_flux(before[2], current[2], before[0], current[0])
        carry = (before[0], current, flux)
        for i in range(start, HALO):
            carry = advance_row(src, store, i, carry, 0 if i == HALO - 1 else None)
        carry = lax.fori_loop(
            HALO, HALO + rows - 1, lambda i, c, src=src, store=store: advance_row(src, store, i, c), carry
        )
        carry = advance_row(src, store, HALO + rows - 1, carry, 2)
        for i in range(HALO + rows, HALO + rows + margin):
            carry = advance_row(src, store, i, carry)

    out_copies = [
        pltpu.make_async_copy(out_v.at[f, b], out.at[:, :, b * LANES : (b + 1) * LANES], out_sem.at[f, b])
        for f, out in enumerate((out_depth, out_first, out_second))
        for b in range(blocks)
    ]
    for copy in out_copies:
        copy.start()
    for d in range(1, flows + 1):

        def sent(c, carry):
            direct(d, c).wait_send()

            @pl.when(relayed(d))
            def _():
                second_leg(d, c).wait_send()

            return carry

        lax.fori_loop(0, SEND_CHUNKS, sent, 0)
    for copy in grid_copies + strip_copies:
        copy.wait_send()
    for copy in out_copies:
        copy.wait()


def body(
    increments, remap_weights, dest_offset, slot_patch, rotation, basis,
    inv_metric_diag, inv_metric_cross, thickness, wind_first, wind_second,
):
    levels, rows, cols = thickness.shape
    lat_rows, top, patch, cells = remap_weights.shape[2:]
    pairs = 3 * levels
    entries = lat_rows * top
    owners, capacity = slot_patch.shape[2:]
    flows = owners - 1
    slots = owners * capacity
    blocks = cols // LANES
    patches = rows * blocks
    per = capacity // SEND_CHUNKS
    ty = lax.axis_index("ty")

    offsets = dest_offset.reshape(entries)
    ids = jnp.arange(entries, dtype=jnp.int32)
    same = (offsets[:, None] == offsets[None, :]) & (ids[None, :] < ids[:, None])
    position = offsets * capacity + jnp.sum(same.astype(jnp.int32), axis=1)
    slot_ids = jnp.arange(slots, dtype=jnp.int32)
    perm = jnp.min(jnp.where(position[None, :] == slot_ids[:, None], ids[None, :], entries), axis=1)
    table = slot_patch[0, 0]
    arrivals = table[1:].reshape(flows, SEND_CHUNKS, per).transpose(1, 0, 2).reshape(-1)
    order = jnp.concatenate([table[0], arrivals])
    match = (order[:, None] == order[None, :]) & (slot_ids[None, :] < slot_ids[:, None])
    prev = jnp.max(jnp.where(match, slot_ids[None, :], -1), axis=1)
    prev = jnp.where(prev < 0, slots, prev)
    patch_ids = jnp.arange(patches, dtype=jnp.int32)
    last = jnp.max(jnp.where(order[None, :] == patch_ids[:, None], slot_ids[None, :], -1), axis=1)
    last = jnp.where(last < 0, slots, last)

    tiles = lax.axis_size("ty") // PANELS
    panel = ty // tiles
    at_low = ty % tiles == 0
    at_high = ty % tiles == tiles - 1
    codes = jnp.stack(
        [
            jnp.where(at_low, rotation[1, (panel + PANELS - 1) % PANELS], 0),
            jnp.where(at_low, rotation[0, panel], 0),
            jnp.where(at_high, rotation[1, panel], 0),
            jnp.where(at_high, rotation[0, (panel + 1) % PANELS], 0),
        ]
    )
    cosine = (codes == 0).astype(jnp.float32) - (codes == 2).astype(jnp.float32)
    sine = (codes == 1).astype(jnp.float32) - (codes == 3).astype(jnp.float32)
    turn = jnp.stack([sine, cosine], axis=1).reshape(-1)

    f32 = jnp.float32
    hrows = rows + 2 * HALO
    packs = -(-3 * rows // GROUPS)
    vmem, dma = pltpu.VMEM, pltpu.SemaphoreType.DMA
    scratch = [
        vmem((W_SLOTS, W_ROWS, top * patch, cells), jnp.bfloat16),
        vmem((pairs, lat_rows, cells), jnp.bfloat16),
        vmem((pairs * W_ROWS, LANES), f32),
        vmem((pairs * W_ROWS, LANES), f32),
        vmem((entries + 1, pairs, LANES), f32),
        vmem((flows, capacity, pairs, LANES), f32),
        vmem((flows, capacity, pairs, LANES), f32),
        vmem((flows, capacity, pairs, LANES), f32),
        vmem((slots + 1, pairs, LANES), f32),
        vmem((3, hrows, blocks + 1, levels, LANES), f32),
        vmem((3, hrows, blocks + 1, levels, LANES), f32),
        vmem((3, hrows, blocks + 1, levels, LANES), f32),
        vmem((4, rows, blocks, levels, LANES), f32),
        vmem((3, blocks, levels, rows, LANES), f32),
        vmem((3, blocks, levels, rows, LANES), f32),
        vmem((3, rows + 16, cols), f32),
        vmem((2, 3, rows + 16, LANES), f32),
        vmem((4, rows, cols), f32),
        vmem((2, packs, levels, LANES), f32),
        vmem((2, packs + 2, levels, LANES), f32),
        dma((W_SLOTS,)),
        dma,
        dma((3 + 3 * blocks,)),
        dma((3, blocks)),
        dma((flows, SEND_CHUNKS)),
        dma((flows, SEND_CHUNKS)),
        dma((flows, SEND_CHUNKS)),
        dma((flows, SEND_CHUNKS)),
        dma((8,)),
        dma((8,)),
        dma((8,)),
        dma((8,)),
    ]
    anywhere = pl.BlockSpec(memory_space=pl.ANY)
    scalars = pl.BlockSpec(memory_space=pltpu.SMEM)
    return pl.pallas_call(
        kernel,
        out_shape=[jax.ShapeDtypeStruct(thickness.shape, f32)] * 3,
        in_specs=[scalars] * 4 + [anywhere] * 8,
        out_specs=[anywhere] * 3,
        scratch_shapes=scratch,
        compiler_params=pltpu.CompilerParams(
            collective_id=0, has_side_effects=True, vmem_limit_bytes=62 * 1024 * 1024
        ),
    )(
        perm, prev, last, turn,
        increments.reshape(pairs, lat_rows, cells),
        remap_weights.reshape(lat_rows, top * patch, cells),
        basis, inv_metric_diag, inv_metric_cross, thickness, wind_first, wind_second,
    )


def solution(mesh):
    tile = P(None, "ty", "tx")
    in_specs = (
        P(None, None, "tx", "ty"),
        P("tx", "ty", None, None, None, None),
        P("tx", "ty", None, None),
        P("tx", "ty", None, None),
        P(),
        tile,
        tile,
        P("ty", "tx"),
        tile,
        tile,
        tile,
    )
    return jax.shard_map(body, mesh=mesh, in_specs=in_specs, out_specs=(tile, tile, tile), check_vma=False)
```

```python
import jax
import jax.numpy as jnp
from jax import lax
from jax.experimental import pallas as pl
from jax.experimental.pallas import tpu as pltpu
from jax.sharding import PartitionSpec as P

MESH = pl.DeviceIdType.MESH
PANELS = 4
STEPS = 4
HALO = 4
COURANT = 0.15
HALF_GRADIENT = 0.15
LANES = 128
GROUPS = 32
NX = 4
SEND_CHUNKS = 6
LAG = 1
EDGE = HALO + 1
ROWS = 4
W_SLOTS = 4
W_ROWS = 16


def kernel(
    offsets, patches, rotation, inc, wts, basis, diag, cross, depth_in, first_in, second_in,
    out_depth, out_first, out_second,
    wbuf, inc_v, half0, half1, term, send, recv, relay, acc, xa, xb, metric, bases,
    state_in, out_v, grid_raw, grid_side, basis_raw, packed, strips, off_v, patch_v, table_v, table,
    w_sem, in_sem, table_sem, field_sem, out_sem, send_sem, recv_sem, relay_send_sem, relay_recv_sem,
    grid_send_sem, grid_recv_sem, halo_send_sem, halo_recv_sem,
):
    tx = lax.axis_index("tx")
    ty = lax.axis_index("ty")
    n_tx = lax.axis_size("tx")
    n_ty = lax.axis_size("ty")
    x = lax.rem(ty, NX)
    odd = lax.rem(tx, 2) == 1
    flows, capacity = send.shape[0], send.shape[1]
    entries = term.shape[0] - 1
    slots = acc.shape[0] - 1
    per = capacity // SEND_CHUNKS
    rows = state_in.shape[3]
    levels = state_in.shape[2]
    blocks = state_in.shape[1]
    w_chunks = wts.shape[0] // W_ROWS

    def dev(dx, dy):
        return (lax.rem(tx + dx + n_tx, n_tx), lax.rem(ty + dy + n_ty, n_ty))

    barrier = pltpu.get_barrier_semaphore()
    partners = [(0, s * d) for d in (1, 2, 3, 4) for s in (1, -1)]
    partners += [(s, d) for s in (1, -1) for d in (-1, 0, 1)]
    for dx, dy in partners:
        pl.semaphore_signal(barrier, inc=1, device_id=dev(dx, dy), device_id_type=MESH)

    def w_copy(chunk, slot):
        return pltpu.make_async_copy(wts.at[pl.ds(chunk * W_ROWS, W_ROWS)], wbuf.at[slot], w_sem.at[slot])

    inc_copy = pltpu.make_async_copy(inc, inc_v, in_sem)
    inc_copy.start()
    for slot in range(W_SLOTS):
        w_copy(slot, slot).start()
    field_copies = [
        pltpu.make_async_copy(diag, grid_raw.at[0:2, 8 : 8 + rows], field_sem.at[0]),
        pltpu.make_async_copy(cross, grid_raw.at[2, 8 : 8 + rows], field_sem.at[1]),
        pltpu.make_async_copy(basis, basis_raw, field_sem.at[2]),
    ]
    for i, field in enumerate((depth_in, first_in, second_in)):
        for b in range(blocks):
            field_copies.append(
                pltpu.make_async_copy(
                    field.at[:, :, b * LANES : (b + 1) * LANES], state_in.at[i, b], field_sem.at[3 + i * blocks + b]
                )
            )
    for copy in field_copies:
        copy.start()

    owners = flows + 1
    square = (LANES, LANES)
    row_id = lax.broadcasted_iota(jnp.int32, square, 0)
    col_id = lax.broadcasted_iota(jnp.int32, square, 1)
    tops, lat_rows = offsets.shape
    off_v[...] = jnp.full(off_v.shape, owners, jnp.int32)
    off_v[0:tops, 0:lat_rows] = offsets[...]
    patch_v[...] = jnp.full(patch_v.shape, -1, jnp.int32)
    patch_v[0:owners, 0:capacity] = patches[...]
    off = [off_v[t : t + 1, :] for t in range(tops)]
    wide = off_v.shape[1]
    hits = [[(off[t] == d).astype(jnp.float32) for t in range(tops)] for d in range(owners)]
    stacked = jnp.concatenate([jnp.broadcast_to(hits[d][t], (8, wide)) for d in range(owners) for t in range(tops)], axis=0)
    before_mask = lax.broadcasted_iota(jnp.int32, (wide, wide), 0) < lax.broadcasted_iota(jnp.int32, (wide, wide), 1)
    counts = jnp.dot(
        stacked.astype(jnp.bfloat16), before_mask.astype(jnp.bfloat16), preferred_element_type=jnp.float32
    )
    place = []
    for t in range(tops):
        rank = jnp.zeros((1, wide), jnp.float32)
        for d in range(owners):
            earlier = sum(counts[8 * (d * tops + u) : 8 * (d * tops + u) + 1] for u in range(tops))
            earlier = earlier + sum(hits[d][u] for u in range(t)) if t else earlier
            rank = rank + hits[d][t] * earlier
        place.append(off[t] * LANES + rank.astype(jnp.int32))
    found = [jnp.zeros((1, LANES), jnp.int32) for _ in range(owners)]
    for t in range(tops):
        for h in range(wide // LANES):
            column = jnp.transpose(jnp.broadcast_to(place[t][:, h * LANES : (h + 1) * LANES], square))
            entry = (row_id + h * LANES) * tops + t - entries
            for d in range(owners):
                hit = jnp.where(column == col_id + d * LANES, entry, 0)
                found[d] = found[d] + jnp.sum(hit, axis=0, keepdims=True)
    for d in range(owners):
        table_v[d : d + 1, :] = found[d] + entries

    def order(d, k):
        if d == 0:
            return jnp.where(k < capacity, k, slots)
        chunk = k // per
        return jnp.where(k < capacity, capacity + (chunk * flows + d - 1) * per + (k - chunk * per), slots)

    column_patch = [jnp.transpose(jnp.broadcast_to(patch_v[d : d + 1, :], square)) for d in range(owners)]
    column_order = [order(d, row_id) for d in range(owners)]
    for d in range(owners):
        mine, target = patch_v[d : d + 1, :], order(d, col_id)
        best = jnp.full(square, -1, jnp.int32)
        for e in range(owners):
            hit = jnp.logical_and(column_patch[e] == mine, column_order[e] < target)
            best = jnp.maximum(best, jnp.where(hit, column_order[e], -1))
        best = jnp.max(best, axis=0, keepdims=True)
        table_v[owners + d : owners + d + 1, :] = jnp.where(best < 0, slots, best)
    for h in range(2):
        best = jnp.full(square, -1, jnp.int32)
        for e in range(owners):
            hit = jnp.logical_and(column_patch[e] == col_id + h * LANES, column_order[e] < slots)
            best = jnp.maximum(best, jnp.where(hit, column_order[e], -1))
        best = jnp.max(best, axis=0, keepdims=True)
        table_v[2 * owners + h : 2 * owners + h + 1, :] = jnp.where(best < 0, slots, best)
    table_copy = pltpu.make_async_copy(table_v, table, table_sem)
    table_copy.start()

    zero_row = jnp.zeros(term.shape[1:], jnp.float32)
    term[entries] = zero_row
    acc[slots] = zero_row

    inc_copy.wait()

    def term_chunk(chunk, carry):
        slot = lax.rem(chunk, W_SLOTS)
        start = pl.multiple_of(chunk * W_ROWS, W_ROWS)
        cells = inc_v[:, pl.ds(start, W_ROWS), :].astype(jnp.float32)
        pairs = cells.shape[0]
        half0[...] = cells[:, :, :LANES].reshape(pairs * W_ROWS, LANES)
        half1[...] = cells[:, :, LANES:].reshape(pairs * W_ROWS, LANES)
        w_copy(chunk, slot).wait()
        for s in range(W_ROWS):
            lhs = jnp.concatenate(
                [half0[pl.ds(s, pairs, stride=W_ROWS), :], half1[pl.ds(s, pairs, stride=W_ROWS), :]], axis=1
            ).astype(jnp.bfloat16)
            product = lax.dot_general(
                lhs, wbuf[slot, s], (((1,), (1,)), ((), ())), preferred_element_type=jnp.float32
            )
            entry = 2 * (start + s)
            term[entry] = product[:, :LANES]
            term[entry + 1] = product[:, LANES:]

        @pl.when(chunk + W_SLOTS < w_chunks)
        def _():
            w_copy(chunk + W_SLOTS, slot).start()

        return carry

    lax.fori_loop(0, w_chunks, term_chunk, 0)

    table_copy.wait()
    pl.semaphore_wait(barrier, len(partners))

    def direct(d, c):
        part = pl.ds(c * per, per)
        return pltpu.make_async_remote_copy(
            send.at[d - 1, part], recv.at[d - 1, part], send_sem.at[d - 1, c], recv_sem.at[d - 1, c],
            device_id=dev(0, d), device_id_type=MESH,
        )

    def first_leg(d, c):
        part = pl.ds(c * per, per)
        return pltpu.make_async_remote_copy(
            send.at[d - 1, part], relay.at[d - 1, part], send_sem.at[d - 1, c], relay_recv_sem.at[d - 1, c],
            device_id=dev(0, NX), device_id_type=MESH,
        )

    def second_leg(d, c):
        part = pl.ds(c * per, per)
        return pltpu.make_async_remote_copy(
            relay.at[d - 1, part], recv.at[d - 1, part], relay_send_sem.at[d - 1, c], recv_sem.at[d - 1, c],
            device_id=dev(0, d - NX), device_id_type=MESH,
        )

    def relayed(d):
        return jnp.logical_and(odd, x + d >= NX)

    def forward(c):
        for d in range(1, flows + 1):

            @pl.when(relayed(d))
            def _():
                first_leg(d, c).wait_recv()
                second_leg(d, c).start()

    def send_chunk(c, carry):
        for d in range(1, flows + 1):

            def gather(i, inner):
                k = c * per + i
                send[d - 1, k] = term[table[d, k]]
                return inner

            lax.fori_loop(0, per, gather, 0, unroll=6)

            @pl.when(relayed(d))
            def _():
                first_leg(d, c).start()

            @pl.when(jnp.logical_not(relayed(d)))
            def _():
                direct(d, c).start()

        @pl.when(c >= LAG)
        def _():
            forward(c - LAG)

        return carry

    lax.fori_loop(0, SEND_CHUNKS, send_chunk, 0)
    for c in range(SEND_CHUNKS - LAG, SEND_CHUNKS):
        forward(c)

    for copy in field_copies:
        copy.wait()

    own = slice(8, 8 + rows)
    low = slice(8, 16)
    high = slice(rows, 8 + rows)
    below = slice(0, 8)
    above = slice(8 + rows, 16 + rows)
    left = slice(0, LANES)
    right = slice((blocks - 1) * LANES, blocks * LANES)
    grid_moves = [
        (grid_raw.at[:, low], grid_raw.at[:, above], (0, -1)),
        (grid_raw.at[:, high], grid_raw.at[:, below], (0, 1)),
        (grid_raw.at[:, own, left], grid_side.at[0, :, own], (-1, 0)),
        (grid_raw.at[:, low, left], grid_side.at[0, :, above], (-1, -1)),
        (grid_raw.at[:, high, left], grid_side.at[0, :, below], (-1, 1)),
        (grid_raw.at[:, own, right], grid_side.at[1, :, own], (1, 0)),
        (grid_raw.at[:, low, right], grid_side.at[1, :, above], (1, -1)),
        (grid_raw.at[:, high, right], grid_side.at[1, :, below], (1, 1)),
    ]
    grid_copies = [
        pltpu.make_async_remote_copy(
            src, dst, grid_send_sem.at[i], grid_recv_sem.at[i], device_id=dev(*to), device_id_type=MESH
        )
        for i, (src, dst, to) in enumerate(grid_moves)
    ]
    for copy in grid_copies:
        copy.start()

    def accumulate_own(i, carry):
        acc[i] = term[table[0, i]] + acc[table[owners, i]]
        return carry

    lax.fori_loop(0, capacity, accumulate_own, 0, unroll=4)

    shape = (levels, LANES)
    lane = lax.broadcasted_iota(jnp.int32, shape, 1)
    keep_right = jnp.where(tx < n_tx - 1, 1.0, 0.0).astype(jnp.float32)
    keep_left = jnp.where(tx > 0, 1.0, 0.0).astype(jnp.float32)

    def spread(block, j):
        return jnp.broadcast_to(block[j : j + 1], shape)

    def spread_basis(t, carry):
        at = pl.ds(pl.multiple_of(t * 8, 8), 8)
        for k in range(4):
            for b in range(blocks):
                block = basis_raw[k, at, b * LANES : (b + 1) * LANES]
                for j in range(8):
                    bases[k, t * 8 + j, b] = spread(block, j)
        return carry

    lax.fori_loop(0, rows // 8, spread_basis, 0)

    for copy in grid_copies:
        copy.wait_recv()

    def spread_metric(t, carry, picks=range(8)):
        at = pl.ds(pl.multiple_of(t * 8, 8), 8)
        base = t * 8 - 8 + EDGE
        for k in range(3):
            for b in range(blocks):
                block = grid_raw[k, at, b * LANES : (b + 1) * LANES]
                for j in picks:
                    metric[k, base + j, b] = spread(block, j)
            side = jnp.where(lane < LANES // 2, grid_side[0, k, at, :] * keep_right, grid_side[1, k, at, :] * keep_left)
            for j in picks:
                metric[k, base + j, blocks] = spread(side, j)
        return carry

    spread_metric(0, 0, range(8 - HALO, 8))
    lax.fori_loop(1, 1 + rows // 8, spread_metric, 0)
    spread_metric(1 + rows // 8, 0, range(HALO))

    def receive_chunk(c, carry):
        for d in range(1, flows + 1):
            direct(d, c).wait_recv()
            base = capacity + (c * flows + d - 1) * per

            def add(i, inner):
                acc[base + i] = recv[d - 1, c * per + i] + acc[table[owners + d, c * per + i]]
                return inner

            lax.fori_loop(0, per, add, 0, unroll=6)
        return carry

    lax.fori_loop(0, SEND_CHUNKS, receive_chunk, 0)

    def regrid(r, carry):
        for b in range(blocks):
            q = r * blocks + b
            patch = acc.at[table[2 * owners + q // LANES, lax.rem(q, LANES)]]
            east, north, thick = patch[0:levels], patch[levels : 2 * levels], patch[2 * levels : 3 * levels]
            at = pl.ds(r, levels, stride=rows)

            def start(i):
                return state_in.at[i, b].reshape(levels * rows, LANES)[at, :]

            xa[0, r + EDGE, b] = start(0) + thick
            xa[1, r + EDGE, b] = start(1) + bases[0, r, b] * east + bases[1, r, b] * north
            xa[2, r + EDGE, b] = start(2) + bases[2, r, b] * east + bases[3, r, b] * north
        return carry

    lax.fori_loop(0, HALO, regrid, 0)
    lax.fori_loop(rows - HALO, rows, regrid, 0)

    def halo_copy(i, src, dst, to):
        return pltpu.make_async_remote_copy(
            src, dst, halo_send_sem.at[i], halo_recv_sem.at[i], device_id=dev(*to), device_id_type=MESH
        )

    row_copies = [
        halo_copy(0, xa.at[:, EDGE : EDGE + HALO, 0:blocks], xa.at[:, EDGE + rows : EDGE + rows + HALO, 0:blocks], (0, -1)),
        halo_copy(1, xa.at[:, EDGE + rows - HALO : EDGE + rows, 0:blocks], xa.at[:, EDGE - HALO : EDGE, 0:blocks], (0, 1)),
    ]
    for copy in row_copies:
        copy.start()

    lax.fori_loop(HALO, rows - HALO, regrid, 0)

    group = lane // HALO
    packs = packed.shape[1]
    for side in range(2):
        for v in range(packs):
            total = jnp.zeros(shape, jnp.float32)
            for g in range(GROUPS):
                item = v * GROUPS + g
                if item >= 3 * rows:
                    break
                edge = xa[item % 3, item // 3 + EDGE, 0 if side == 0 else blocks - 1]
                shift = (HALO * g + (HALO if side else 0)) % LANES
                moved = pltpu.roll(edge, shift, 1) if shift else edge
                total = jnp.where(group == g, moved, total)
            packed[side, v] = total

    strip_copies = []
    for side, dx in ((0, -1), (1, 1)):
        strip_copies += [
            halo_copy(2 + 3 * side, packed.at[side], strips.at[side, 0:packs], (dx, 0)),
            halo_copy(3 + 3 * side, packed.at[side, 0:1], strips.at[side, packs + 1 : packs + 2], (dx, -1)),
            halo_copy(4 + 3 * side, packed.at[side, packs - 1 : packs], strips.at[side, packs : packs + 1], (dx, 1)),
        ]
    for copy in strip_copies:
        copy.start()
    for copy in strip_copies:
        copy.wait_recv()

    for r in range(-HALO, rows + HALO):
        for f in range(3):
            item = 3 * (r % rows) + f
            g = item % GROUPS
            v = item // GROUPS
            if r < 0:
                v = packs
            elif r >= rows:
                v = packs + 1
            from_right = pltpu.roll(strips[0, v], (LANES - HALO * g) % LANES, 1) if g else strips[0, v]
            from_left = pltpu.roll(strips[1, v], (LANES - HALO - HALO * g) % LANES, 1) if g < GROUPS - 1 else strips[1, v]
            xa[f, r + EDGE, blocks] = jnp.where(
                lane < HALO,
                from_right * keep_right,
                jnp.where(lane >= LANES - HALO, from_left * keep_left, 0.0),
            )
    ring = blocks + 1
    is_first = lane == 0
    is_last = lane == LANES - 1
    one = jnp.ones(shape, jnp.float32)
    wall_right = jnp.where(is_last, keep_right, one)
    wall_left = jnp.where(is_last, keep_left, one)
    wall_right_halo = jnp.where(is_first, keep_right, one)
    wall_left_tile = jnp.where(is_first, keep_left, one)

    def from_next(values):
        rolled = [pltpu.roll(v, LANES - 1, 1) for v in values]
        return [jnp.where(is_last, rolled[(b + 1) % ring], rolled[b]) for b in range(ring)]

    def from_before(values):
        rolled = [pltpu.roll(v, 1, 1) for v in values]
        return [jnp.where(is_first, rolled[(b - 1) % ring], rolled[b]) for b in range(ring)]

    def load(src, i):
        depth, con_first, con_second = [], [], []
        for b in range(ring):
            first, second = src[1, i, b], src[2, i, b]
            depth.append(src[0, i, b])
            con_first.append(metric[0, i, b] * first + metric[2, i, b] * second)
            con_second.append(metric[2, i, b] * first + metric[1, i, b] * second)
        return depth, con_first, con_second

    def row_flux(second_low, second_high, depth_low, depth_high):
        out = []
        for b in range(ring):
            face = 0.5 * (second_low[b] + second_high[b])
            out.append(jnp.maximum(face, 0.0) * depth_low[b] + jnp.minimum(face, 0.0) * depth_high[b])
        return out

    tiles = n_ty // PANELS
    panel = ty // tiles
    place_in_panel = lax.rem(ty, tiles)

    def joint(present, code):
        code = jnp.where(present, code, 0)

        def equals(value):
            return jnp.where(code == value, 1.0, 0.0).astype(jnp.float32)

        return equals(1) - equals(3), equals(0) - equals(2)

    low_joint, high_joint = place_in_panel == 0, place_in_panel == tiles - 1
    low_above = joint(low_joint, rotation[1, lax.rem(panel + PANELS - 1, PANELS)])
    low_below = joint(low_joint, rotation[0, panel])
    high_above = joint(high_joint, rotation[1, panel])
    high_below = joint(high_joint, rotation[0, lax.rem(panel + 1, PANELS)])
    groups = rows // ROWS

    def pick(group, low_turn, high_turn):
        return [
            jnp.where(group == 0, low_turn[k], jnp.where(group == groups, high_turn[k], float(k))) for k in range(2)
        ]

    def turned(turn, con_first, con_second):
        return [turn[0] * con_first[b] + turn[1] * con_second[b] for b in range(ring)]

    def flux_into(src, group):
        i = EDGE - ROWS + group * ROWS
        low, high = load(src, i - 1), load(src, i)
        turn = pick(group - 1, low_below, high_below)
        return row_flux(turned(turn, low[1], low[2]), high[2], low[0], high[0])

    def advance_group(src, store, group, flux_below):
        i = EDGE - ROWS + group * ROWS
        depth_before = [src[0, i - 1, b] for b in range(ring)]
        current = load(src, i)
        for j in range(ROWS):
            depth, con_first, con_second = current
            after = load(src, i + j + 1)
            depth_after, first_after, second_after = after
            if j < ROWS - 1:
                flux_above = row_flux(con_second, second_after, depth, depth_after)
                flux_next = flux_above
            else:
                turn_above = pick(group, low_above, high_above)
                turn_below = pick(group, low_below, high_below)
                flux_above = row_flux(con_second, turned(turn_above, first_after, second_after), depth, depth_after)
                flux_next = row_flux(turned(turn_below, con_first, con_second), second_after, depth, depth_after)
            depth_right, first_right = from_next(depth), from_next(con_first)
            depth_left, first_left = from_before(depth), from_before(con_first)
            for b in range(ring):
                face = 0.5 * (con_first[b] + first_right[b])
                if b == blocks - 1:
                    face = face * wall_right
                if b == blocks:
                    face = face * wall_left
                flux_right = jnp.maximum(face, 0.0) * depth[b] + jnp.minimum(face, 0.0) * depth_right[b]
                face = 0.5 * (con_first[b] + first_left[b])
                if b == blocks:
                    face = face * wall_right_halo
                if b == 0:
                    face = face * wall_left_tile
                flux_left = jnp.maximum(face, 0.0) * depth_left[b] + jnp.minimum(face, 0.0) * depth[b]
                new_depth = depth[b] - COURANT * ((flux_right - flux_left) + (flux_above[b] - flux_below[b]))
                new_first = src[1, i + j, b] - HALF_GRADIENT * (depth_right[b] - depth_left[b])
                new_second = src[2, i + j, b] - HALF_GRADIENT * (depth_after[b] - depth_before[b])
                store(i + j, b, (new_depth, new_first, new_second))
            depth_before, current, flux_below = depth, after, flux_next
        return flux_below

    for step in range(STEPS):
        src, dst = (xa, xb) if step % 2 == 0 else (xb, xa)

        def store_state(i, b, values, dst=dst):
            for f in range(3):
                dst[f, i, b] = values[f]

        def store_out(i, b, values):
            if b < blocks:
                for f in range(3):
                    out_v.at[f, b].reshape(levels * rows, LANES)[pl.ds(i - EDGE, levels, stride=rows), :] = values[f]

        store = store_out if step == STEPS - 1 else store_state

        def sweep(first, end, src=src, store=store):
            lax.fori_loop(
                first, end, lambda g, flux: tuple(advance_group(src, store, g, flux)), tuple(flux_into(src, first))
            )

        if step == 0:
            sweep(2, groups)
            for copy in row_copies:
                copy.wait_recv()
            sweep(0, 2)
            sweep(groups, groups + 2)
            for copy in row_copies:
                copy.wait_send()
        elif step < STEPS - 1:
            sweep(0, groups + 2)
        else:
            sweep(1, groups + 1)

    out_copies = [
        pltpu.make_async_copy(out_v.at[f, b], out.at[:, :, b * LANES : (b + 1) * LANES], out_sem.at[f, b])
        for f, out in enumerate((out_depth, out_first, out_second))
        for b in range(blocks)
    ]
    for copy in out_copies:
        copy.start()
    for d in range(1, flows + 1):

        def sent(c, carry):
            direct(d, c).wait_send()

            @pl.when(relayed(d))
            def _():
                second_leg(d, c).wait_send()

            return carry

        lax.fori_loop(0, SEND_CHUNKS, sent, 0)
    for copy in grid_copies + strip_copies:
        copy.wait_send()
    for copy in out_copies:
        copy.wait()


def body(
    increments, remap_weights, dest_offset, slot_patch, rotation, basis,
    inv_metric_diag, inv_metric_cross, thickness, wind_first, wind_second,
):
    levels, rows, cols = thickness.shape
    lat_rows, top, patch, cells = remap_weights.shape[2:]
    pairs = 3 * levels
    entries = lat_rows * top
    owners, capacity = slot_patch.shape[2:]
    flows = owners - 1
    slots = owners * capacity
    blocks = cols // LANES
    f32 = jnp.float32
    hrows = rows + 2 * EDGE
    packs = -(-3 * rows // GROUPS)
    vmem, dma = pltpu.VMEM, pltpu.SemaphoreType.DMA
    scratch = [
        vmem((W_SLOTS, W_ROWS, top * patch, cells), jnp.bfloat16),
        vmem((pairs, lat_rows, cells), jnp.bfloat16),
        vmem((pairs * W_ROWS, LANES), f32),
        vmem((pairs * W_ROWS, LANES), f32),
        vmem((entries + 1, pairs, LANES), f32),
        vmem((flows, capacity, pairs, LANES), f32),
        vmem((flows, capacity, pairs, LANES), f32),
        vmem((flows, capacity, pairs, LANES), f32),
        vmem((slots + 1, pairs, LANES), f32),
        vmem((3, hrows, blocks + 1, levels, LANES), f32),
        vmem((3, hrows, blocks + 1, levels, LANES), f32),
        vmem((3, hrows, blocks + 1, levels, LANES), f32),
        vmem((4, rows, blocks, levels, LANES), f32),
        vmem((3, blocks, levels, rows, LANES), f32),
        vmem((3, blocks, levels, rows, LANES), f32),
        vmem((3, rows + 16, cols), f32),
        vmem((2, 3, rows + 16, LANES), f32),
        vmem((4, rows, cols), f32),
        vmem((2, packs, levels, LANES), f32),
        vmem((2, packs + 2, levels, LANES), f32),
        vmem((8, 2 * LANES), jnp.int32),
        vmem((8, LANES), jnp.int32),
        vmem((16, LANES), jnp.int32),
        pltpu.SMEM((16, LANES), jnp.int32),
        dma((W_SLOTS,)),
        dma,
        dma,
        dma((3 + 3 * blocks,)),
        dma((3, blocks)),
        dma((flows, SEND_CHUNKS)),
        dma((flows, SEND_CHUNKS)),
        dma((flows, SEND_CHUNKS)),
        dma((flows, SEND_CHUNKS)),
        dma((8,)),
        dma((8,)),
        dma((8,)),
        dma((8,)),
    ]
    anywhere = pl.BlockSpec(memory_space=pl.ANY)
    on_chip = pl.BlockSpec(memory_space=pltpu.VMEM)
    moved = pl.pallas_call(
        kernel,
        out_shape=[jax.ShapeDtypeStruct(thickness.shape, f32)] * 3,
        in_specs=[on_chip, on_chip, pl.BlockSpec(memory_space=pltpu.SMEM)] + [anywhere] * 8,
        out_specs=[anywhere] * 3,
        scratch_shapes=scratch,
        compiler_params=pltpu.CompilerParams(
            collective_id=0, has_side_effects=True, vmem_limit_bytes=62 * 1024 * 1024
        ),
    )(
        dest_offset[0, 0].T, slot_patch[0, 0], rotation,
        increments.reshape(pairs, lat_rows, cells),
        remap_weights.reshape(lat_rows, top * patch, cells),
        basis, inv_metric_diag, inv_metric_cross, thickness, wind_first, wind_second,
    )
    spec = pl.BlockSpec((levels // 4, rows, cols), lambda i: (i, 0, 0))
    return tuple(
        pl.pallas_call(
            copy_kernel,
            out_shape=[jax.ShapeDtypeStruct(thickness.shape, f32)] * 3,
            grid=(4,),
            in_specs=[spec] * 3,
            out_specs=[spec] * 3,
        )(*moved)
    )


def copy_kernel(depth, first, second, out_depth, out_first, out_second):
    out_depth[...] = depth[...]
    out_first[...] = first[...]
    out_second[...] = second[...]


def solution(mesh):
    tile = P(None, "ty", "tx")
    in_specs = (
        P(None, None, "tx", "ty"),
        P("tx", "ty", None, None, None, None),
        P("tx", "ty", None, None),
        P("tx", "ty", None, None),
        P(),
        tile,
        tile,
        P("ty", "tx"),
        tile,
        tile,
        tile,
    )
    return jax.shard_map(body, mesh=mesh, in_specs=in_specs, out_specs=(tile, tile, tile), check_vma=False)
```

```python
import jax
import jax.numpy as jnp
from jax import lax
from jax.experimental import pallas as pl
from jax.experimental.pallas import tpu as pltpu
from jax.sharding import PartitionSpec as P

MESH = pl.DeviceIdType.MESH
PANELS = 4
STEPS = 4
HALO = 4
COURANT = 0.15
HALF_GRADIENT = 0.15
FACE_SCALE = 0.5 * COURANT
LANES = 128
GROUPS = 16
NX = 4
SEND_CHUNKS = 6
LAG = 1
EDGE = HALO + 1
ROWS = 4
W_SLOTS = 4
W_ROWS = 16


def kernel(
    offsets, patches, rotation, inc, wts, basis, diag, cross, depth_in, first_in, second_in,
    out_depth, out_first, out_second,
    wbuf, inc_v, half0, half1, term, send, recv, relay, acc, xa, xb, metric, bases,
    state_in, out_v, grid_raw, grid_side, basis_raw, packed, strips, off_v, patch_v, table_v, table,
    w_sem, in_sem, table_sem, field_sem, out_sem, send_sem, recv_sem, relay_send_sem, relay_recv_sem,
    grid_send_sem, grid_recv_sem, halo_send_sem, halo_recv_sem,
):
    tx = lax.axis_index("tx")
    ty = lax.axis_index("ty")
    n_tx = lax.axis_size("tx")
    n_ty = lax.axis_size("ty")
    x = lax.rem(ty, NX)
    odd = lax.rem(tx, 2) == 1
    flows, capacity = send.shape[0], send.shape[1]
    entries = term.shape[0] - 1
    slots = acc.shape[0] - 1
    per = capacity // SEND_CHUNKS
    rows = state_in.shape[3]
    levels = state_in.shape[2]
    blocks = state_in.shape[1]
    w_chunks = wts.shape[0] // W_ROWS

    def dev(dx, dy):
        return (lax.rem(tx + dx + n_tx, n_tx), lax.rem(ty + dy + n_ty, n_ty))

    barrier = pltpu.get_barrier_semaphore()
    partners = [(0, s * d) for d in (1, 2, 3, 4) for s in (1, -1)]
    partners += [(s, d) for s in (1, -1) for d in (-1, 0, 1)]
    for dx, dy in partners:
        pl.semaphore_signal(barrier, inc=1, device_id=dev(dx, dy), device_id_type=MESH)

    def w_copy(chunk, slot):
        return pltpu.make_async_copy(wts.at[pl.ds(chunk * W_ROWS, W_ROWS)], wbuf.at[slot], w_sem.at[slot])

    inc_copy = pltpu.make_async_copy(inc, inc_v, in_sem)
    inc_copy.start()
    for slot in range(W_SLOTS):
        w_copy(slot, slot).start()
    field_copies = [
        pltpu.make_async_copy(diag, grid_raw.at[0:2, 8 : 8 + rows], field_sem.at[0]),
        pltpu.make_async_copy(cross, grid_raw.at[2, 8 : 8 + rows], field_sem.at[1]),
        pltpu.make_async_copy(basis, basis_raw, field_sem.at[2]),
    ]
    for i, field in enumerate((depth_in, first_in, second_in)):
        for b in range(blocks):
            field_copies.append(
                pltpu.make_async_copy(
                    field.at[:, :, b * LANES : (b + 1) * LANES], state_in.at[i, b], field_sem.at[3 + i * blocks + b]
                )
            )
    owners = flows + 1
    square = (LANES, LANES)
    row_id = lax.broadcasted_iota(jnp.int32, square, 0)
    col_id = lax.broadcasted_iota(jnp.int32, square, 1)
    tops, lat_rows = offsets.shape
    off_v[...] = jnp.full(off_v.shape, owners, jnp.int32)
    off_v[0:tops, 0:lat_rows] = offsets[...]
    patch_v[...] = jnp.full(patch_v.shape, -1, jnp.int32)
    patch_v[0:owners, 0:capacity] = patches[...]
    off = [off_v[t : t + 1, :] for t in range(tops)]
    wide = off_v.shape[1]
    hits = [[(off[t] == d).astype(jnp.float32) for t in range(tops)] for d in range(owners)]
    stacked = jnp.concatenate([jnp.broadcast_to(hits[d][t], (8, wide)) for d in range(owners) for t in range(tops)], axis=0)
    before_mask = lax.broadcasted_iota(jnp.int32, (wide, wide), 0) < lax.broadcasted_iota(jnp.int32, (wide, wide), 1)
    counts = jnp.dot(
        stacked.astype(jnp.bfloat16), before_mask.astype(jnp.bfloat16), preferred_element_type=jnp.float32
    )
    place = []
    for t in range(tops):
        rank = jnp.zeros((1, wide), jnp.float32)
        for d in range(owners):
            earlier = sum(counts[8 * (d * tops + u) : 8 * (d * tops + u) + 1] for u in range(tops))
            earlier = earlier + sum(hits[d][u] for u in range(t)) if t else earlier
            rank = rank + hits[d][t] * earlier
        place.append(off[t] * LANES + rank.astype(jnp.int32))
    found = [jnp.zeros((1, LANES), jnp.int32) for _ in range(owners)]
    for t in range(tops):
        for h in range(wide // LANES):
            column = jnp.transpose(jnp.broadcast_to(place[t][:, h * LANES : (h + 1) * LANES], square))
            entry = (row_id + h * LANES) * tops + t - entries
            for d in range(owners):
                hit = jnp.where(column == col_id + d * LANES, entry, 0)
                found[d] = found[d] + jnp.sum(hit, axis=0, keepdims=True)
    for d in range(owners):
        table_v[d : d + 1, :] = found[d] + entries

    def order(d, k):
        if d == 0:
            return jnp.where(k < capacity, k, slots)
        chunk = k // per
        return jnp.where(k < capacity, capacity + (chunk * flows + d - 1) * per + (k - chunk * per), slots)

    column_patch = [jnp.transpose(jnp.broadcast_to(patch_v[d : d + 1, :], square)) for d in range(owners)]
    column_order = [order(d, row_id) for d in range(owners)]
    for d in range(owners):
        mine, target = patch_v[d : d + 1, :], order(d, col_id)
        best = jnp.full(square, -1, jnp.int32)
        for e in range(owners):
            hit = jnp.logical_and(column_patch[e] == mine, column_order[e] < target)
            best = jnp.maximum(best, jnp.where(hit, column_order[e], -1))
        best = jnp.max(best, axis=0, keepdims=True)
        table_v[owners + d : owners + d + 1, :] = jnp.where(best < 0, slots, best)
    for h in range(2):
        best = jnp.full(square, -1, jnp.int32)
        for e in range(owners):
            hit = jnp.logical_and(column_patch[e] == col_id + h * LANES, column_order[e] < slots)
            best = jnp.maximum(best, jnp.where(hit, column_order[e], -1))
        best = jnp.max(best, axis=0, keepdims=True)
        table_v[2 * owners + h : 2 * owners + h + 1, :] = jnp.where(best < 0, slots, best)
    table_copy = pltpu.make_async_copy(table_v, table, table_sem)
    table_copy.start()

    zero_row = jnp.zeros(term.shape[1:], jnp.float32)
    term[entries] = zero_row
    acc[slots] = zero_row

    inc_copy.wait()

    def term_chunk(chunk, carry):
        slot = lax.rem(chunk, W_SLOTS)
        start = pl.multiple_of(chunk * W_ROWS, W_ROWS)
        cells = inc_v[:, pl.ds(start, W_ROWS), :].astype(jnp.float32)
        pairs = cells.shape[0]
        half0[...] = cells[:, :, :LANES].reshape(pairs * W_ROWS, LANES)
        half1[...] = cells[:, :, LANES:].reshape(pairs * W_ROWS, LANES)
        w_copy(chunk, slot).wait()
        for s in range(W_ROWS):
            lhs = jnp.concatenate(
                [half0[pl.ds(s, pairs, stride=W_ROWS), :], half1[pl.ds(s, pairs, stride=W_ROWS), :]], axis=1
            ).astype(jnp.bfloat16)
            product = lax.dot_general(
                lhs, wbuf[slot, s], (((1,), (1,)), ((), ())), preferred_element_type=jnp.float32
            )
            entry = 2 * (start + s)
            term[entry] = product[:, :LANES]
            term[entry + 1] = product[:, LANES:]

        @pl.when(chunk + W_SLOTS < w_chunks)
        def _():
            w_copy(chunk + W_SLOTS, slot).start()

        return carry

    lax.fori_loop(0, w_chunks, term_chunk, 0)
    for copy in field_copies:
        copy.start()

    table_copy.wait()
    pl.semaphore_wait(barrier, len(partners))

    def direct(d, c):
        part = pl.ds(c * per, per)
        return pltpu.make_async_remote_copy(
            send.at[d - 1, part], recv.at[d - 1, part], send_sem.at[d - 1, c], recv_sem.at[d - 1, c],
            device_id=dev(0, d), device_id_type=MESH,
        )

    def first_leg(d, c):
        part = pl.ds(c * per, per)
        return pltpu.make_async_remote_copy(
            send.at[d - 1, part], relay.at[d - 1, part], send_sem.at[d - 1, c], relay_recv_sem.at[d - 1, c],
            device_id=dev(0, NX), device_id_type=MESH,
        )

    def second_leg(d, c):
        part = pl.ds(c * per, per)
        return pltpu.make_async_remote_copy(
            relay.at[d - 1, part], recv.at[d - 1, part], relay_send_sem.at[d - 1, c], recv_sem.at[d - 1, c],
            device_id=dev(0, d - NX), device_id_type=MESH,
        )

    def relayed(d):
        return jnp.logical_and(odd, x + d >= NX)

    def forward(c):
        for d in range(1, flows + 1):

            @pl.when(relayed(d))
            def _():
                first_leg(d, c).wait_recv()
                second_leg(d, c).start()

    def send_chunk(c, carry):
        for d in range(1, flows + 1):

            def gather(i, inner):
                k = c * per + i
                send[d - 1, k] = term[table[d, k]]
                return inner

            lax.fori_loop(0, per, gather, 0, unroll=6)

            @pl.when(relayed(d))
            def _():
                first_leg(d, c).start()

            @pl.when(jnp.logical_not(relayed(d)))
            def _():
                direct(d, c).start()

        @pl.when(c >= LAG)
        def _():
            forward(c - LAG)

        return carry

    lax.fori_loop(0, SEND_CHUNKS, send_chunk, 0)
    for c in range(SEND_CHUNKS - LAG, SEND_CHUNKS):
        forward(c)

    for copy in field_copies:
        copy.wait()

    own = slice(8, 8 + rows)
    low = slice(8, 16)
    high = slice(rows, 8 + rows)
    below = slice(0, 8)
    above = slice(8 + rows, 16 + rows)
    left = slice(0, LANES)
    right = slice((blocks - 1) * LANES, blocks * LANES)
    grid_moves = [
        (grid_raw.at[:, low], grid_raw.at[:, above], (0, -1)),
        (grid_raw.at[:, high], grid_raw.at[:, below], (0, 1)),
        (grid_raw.at[:, own, left], grid_side.at[0, :, own], (-1, 0)),
        (grid_raw.at[:, low, left], grid_side.at[0, :, above], (-1, -1)),
        (grid_raw.at[:, high, left], grid_side.at[0, :, below], (-1, 1)),
        (grid_raw.at[:, own, right], grid_side.at[1, :, own], (1, 0)),
        (grid_raw.at[:, low, right], grid_side.at[1, :, above], (1, -1)),
        (grid_raw.at[:, high, right], grid_side.at[1, :, below], (1, 1)),
    ]
    grid_copies = [
        pltpu.make_async_remote_copy(
            src, dst, grid_send_sem.at[i], grid_recv_sem.at[i], device_id=dev(*to), device_id_type=MESH
        )
        for i, (src, dst, to) in enumerate(grid_moves)
    ]
    for copy in grid_copies:
        copy.start()

    def accumulate_own(i, carry):
        acc[i] = term[table[0, i]] + acc[table[owners, i]]
        return carry

    lax.fori_loop(0, capacity, accumulate_own, 0, unroll=4)

    shape = (levels, LANES)
    lane = lax.broadcasted_iota(jnp.int32, shape, 1)
    keep_right = jnp.where(tx < n_tx - 1, 1.0, 0.0).astype(jnp.float32)
    keep_left = jnp.where(tx > 0, 1.0, 0.0).astype(jnp.float32)

    def spread(block, j):
        return jnp.broadcast_to(block[j : j + 1], shape)

    def spread_basis(t, carry):
        at = pl.ds(pl.multiple_of(t * 8, 8), 8)
        for k in range(4):
            for b in range(blocks):
                block = basis_raw[k, at, b * LANES : (b + 1) * LANES]
                for j in range(8):
                    bases[k, t * 8 + j, b] = spread(block, j)
        return carry

    lax.fori_loop(0, rows // 8, spread_basis, 0)

    for copy in grid_copies:
        copy.wait_recv()

    def spread_metric(t, carry, picks=range(8)):
        at = pl.ds(pl.multiple_of(t * 8, 8), 8)
        base = t * 8 - 8 + EDGE
        for k in range(3):
            for b in range(blocks):
                block = grid_raw[k, at, b * LANES : (b + 1) * LANES]
                for j in picks:
                    metric[k, base + j, b] = spread(block, j) * FACE_SCALE
            side = jnp.where(lane < LANES // 2, grid_side[0, k, at, :] * (keep_right * FACE_SCALE), grid_side[1, k, at, :] * (keep_left * FACE_SCALE))
            for j in picks:
                metric[k, base + j, blocks] = spread(side, j)
        return carry

    spread_metric(0, 0, range(8 - HALO, 8))
    lax.fori_loop(1, 1 + rows // 8, spread_metric, 0)
    spread_metric(1 + rows // 8, 0, range(HALO))

    def receive_chunk(c, carry):
        for d in range(1, flows + 1):
            direct(d, c).wait_recv()
            base = capacity + (c * flows + d - 1) * per

            def add(i, inner):
                acc[base + i] = recv[d - 1, c * per + i] + acc[table[owners + d, c * per + i]]
                return inner

            lax.fori_loop(0, per, add, 0, unroll=6)
        return carry

    lax.fori_loop(0, SEND_CHUNKS, receive_chunk, 0)

    def regrid(r, carry):
        for b in range(blocks):
            q = r * blocks + b
            patch = acc.at[table[2 * owners + q // LANES, lax.rem(q, LANES)]]
            east, north, thick = patch[0:levels], patch[levels : 2 * levels], patch[2 * levels : 3 * levels]
            at = pl.ds(r, levels, stride=rows)

            def start(i):
                return state_in.at[i, b].reshape(levels * rows, LANES)[at, :]

            xa[0, r + EDGE, b] = start(0) + thick
            xa[1, r + EDGE, b] = start(1) + bases[0, r, b] * east + bases[1, r, b] * north
            xa[2, r + EDGE, b] = start(2) + bases[2, r, b] * east + bases[3, r, b] * north
        return carry

    lax.fori_loop(0, HALO, regrid, 0, unroll=4)
    lax.fori_loop(rows - HALO, rows, regrid, 0, unroll=4)

    def halo_copy(i, src, dst, to):
        return pltpu.make_async_remote_copy(
            src, dst, halo_send_sem.at[i], halo_recv_sem.at[i], device_id=dev(*to), device_id_type=MESH
        )

    row_copies = [
        halo_copy(0, xa.at[:, EDGE : EDGE + HALO, 0:blocks], xa.at[:, EDGE + rows : EDGE + rows + HALO, 0:blocks], (0, -1)),
        halo_copy(1, xa.at[:, EDGE + rows - HALO : EDGE + rows, 0:blocks], xa.at[:, EDGE - HALO : EDGE, 0:blocks], (0, 1)),
    ]
    for copy in row_copies:
        copy.start()

    lax.fori_loop(HALO, rows - HALO, regrid, 0, unroll=4)

    group = lax.rem(lane + HALO, LANES) // (2 * HALO)
    packs = packed.shape[0]
    for v in range(packs):
        total = jnp.zeros(shape, jnp.float32)
        for g in range(GROUPS):
            item = v * GROUPS + g
            f, i = item % 3, item // 3 + EDGE
            edges = jnp.where(lane < LANES // 2, xa[f, i, 0], xa[f, i, blocks - 1])
            moved = pltpu.roll(edges, 2 * HALO * g, 1) if g else edges
            total = jnp.where(group == g, moved, total)
        packed[v] = total

    strip_copies = []
    for side, dx in ((0, -1), (1, 1)):
        strip_copies += [
            halo_copy(2 + 3 * side, packed, strips.at[side, 0:packs], (dx, 0)),
            halo_copy(3 + 3 * side, packed.at[0:1], strips.at[side, packs + 1 : packs + 2], (dx, -1)),
            halo_copy(4 + 3 * side, packed.at[packs - 1 : packs], strips.at[side, packs : packs + 1], (dx, 1)),
        ]
    for copy in strip_copies:
        copy.start()
    for copy in strip_copies:
        copy.wait_recv()

    low_half = lax.rem(lane // HALO, 2) == 0
    halos = [
        jnp.where(low_half, strips[0, v] * keep_right, strips[1, v] * keep_left) for v in range(packs + 2)
    ]
    for r in range(-HALO, rows + HALO):
        for f in range(3):
            item = 3 * (r % rows) + f
            g = item % GROUPS
            v = packs if r < 0 else packs + 1 if r >= rows else item // GROUPS
            xa[f, r + EDGE, blocks] = pltpu.roll(halos[v], LANES - 2 * HALO * g, 1) if g else halos[v]

    ring = blocks + 1
    is_first = lane == 0
    is_last = lane == LANES - 1
    one = jnp.ones(shape, jnp.float32)
    wall_right = jnp.where(is_last, keep_right, one)
    wall_left = jnp.where(is_last, keep_left, one)
    wall_right_halo = jnp.where(is_first, keep_right, one)
    wall_left_tile = jnp.where(is_first, keep_left, one)

    def from_next(values):
        rolled = [pltpu.roll(v, LANES - 1, 1) for v in values]
        return [jnp.where(is_last, rolled[(b + 1) % ring], rolled[b]) for b in range(ring)]

    def from_before(values):
        rolled = [pltpu.roll(v, 1, 1) for v in values]
        return [jnp.where(is_first, rolled[(b - 1) % ring], rolled[b]) for b in range(ring)]

    def load(src, i):
        depth, con_first, con_second = [], [], []
        for b in range(ring):
            first, second = src[1, i, b], src[2, i, b]
            depth.append(src[0, i, b])
            con_first.append(metric[0, i, b] * first + metric[2, i, b] * second)
            con_second.append(metric[2, i, b] * first + metric[1, i, b] * second)
        return depth, con_first, con_second

    def upwind(face, depth_low, depth_high):
        return face * jnp.where(face > 0.0, depth_low, depth_high)

    def row_flux(second_low, second_high, depth_low, depth_high):
        out = []
        for b in range(ring):
            out.append(upwind(second_low[b] + second_high[b], depth_low[b], depth_high[b]))
        return out

    tiles = n_ty // PANELS
    panel = ty // tiles
    place_in_panel = lax.rem(ty, tiles)

    def joint(present, code):
        code = jnp.where(present, code, 0)

        def equals(value):
            return jnp.where(code == value, 1.0, 0.0).astype(jnp.float32)

        return equals(1) - equals(3), equals(0) - equals(2)

    low_joint, high_joint = place_in_panel == 0, place_in_panel == tiles - 1
    low_above = joint(low_joint, rotation[1, lax.rem(panel + PANELS - 1, PANELS)])
    low_below = joint(low_joint, rotation[0, panel])
    high_above = joint(high_joint, rotation[1, panel])
    high_below = joint(high_joint, rotation[0, lax.rem(panel + 1, PANELS)])
    groups = rows // ROWS

    def pick(group, low_turn, high_turn):
        return [
            jnp.where(group == 0, low_turn[k], jnp.where(group == groups, high_turn[k], float(k))) for k in range(2)
        ]

    def turned(turn, con_first, con_second):
        return [turn[0] * con_first[b] + turn[1] * con_second[b] for b in range(ring)]

    def flux_into(src, group):
        i = EDGE - ROWS + group * ROWS
        low, high = load(src, i - 1), load(src, i)
        turn = pick(group - 1, low_below, high_below)
        return row_flux(turned(turn, low[1], low[2]), high[2], low[0], high[0])

    def advance_group(src, store, group, flux_below):
        i = EDGE - ROWS + group * ROWS
        depth_before = [src[0, i - 1, b] for b in range(ring)]
        current = load(src, i)
        for j in range(ROWS):
            depth, con_first, con_second = current
            after = load(src, i + j + 1)
            depth_after, first_after, second_after = after
            if j < ROWS - 1:
                flux_above = row_flux(con_second, second_after, depth, depth_after)
                flux_next = flux_above
            else:
                turn_above = pick(group, low_above, high_above)
                turn_below = pick(group, low_below, high_below)
                flux_above = row_flux(con_second, turned(turn_above, first_after, second_after), depth, depth_after)
                flux_next = row_flux(turned(turn_below, con_first, con_second), second_after, depth, depth_after)
            depth_right, first_right = from_next(depth), from_next(con_first)
            depth_left, first_left = from_before(depth), from_before(con_first)
            for b in range(ring):
                face = con_first[b] + first_right[b]
                if b == blocks - 1:
                    face = face * wall_right
                if b == blocks:
                    face = face * wall_left
                flux_right = upwind(face, depth[b], depth_right[b])
                face = con_first[b] + first_left[b]
                if b == blocks:
                    face = face * wall_right_halo
                if b == 0:
                    face = face * wall_left_tile
                flux_left = upwind(face, depth_left[b], depth[b])
                new_depth = depth[b] - ((flux_right - flux_left) + (flux_above[b] - flux_below[b]))
                new_first = src[1, i + j, b] - HALF_GRADIENT * (depth_right[b] - depth_left[b])
                new_second = src[2, i + j, b] - HALF_GRADIENT * (depth_after[b] - depth_before[b])
                store(i + j, b, (new_depth, new_first, new_second))
            depth_before, current, flux_below = depth, after, flux_next
        return flux_below

    for step in range(STEPS):
        src, dst = (xa, xb) if step % 2 == 0 else (xb, xa)

        def store_state(i, b, values, dst=dst):
            for f in range(3):
                dst[f, i, b] = values[f]

        def store_out(i, b, values):
            if b < blocks:
                for f in range(3):
                    out_v.at[f, b].reshape(levels * rows, LANES)[pl.ds(i - EDGE, levels, stride=rows), :] = values[f]

        store = store_out if step == STEPS - 1 else store_state

        def sweep(first, end, src=src, store=store):
            lax.fori_loop(
                first, end, lambda g, flux: tuple(advance_group(src, store, g, flux)), tuple(flux_into(src, first))
            )

        if step == 0:
            sweep(2, groups)
            for copy in row_copies:
                copy.wait_recv()
            sweep(0, 2)
            sweep(groups, groups + 2)
            for copy in row_copies:
                copy.wait_send()
        elif step < STEPS - 1:
            sweep(0, groups + 2)
        else:
            out_copies = []
            half = rows // 2
            for part in range(2):
                sweep(1 + part * groups // 2, 1 + (part + 1) * groups // 2)
                span = slice(part * half, (part + 1) * half)
                copies = [
                    pltpu.make_async_copy(
                        out_v.at[f, b, :, span], out.at[:, span, b * LANES : (b + 1) * LANES], out_sem.at[part, f, b]
                    )
                    for f, out in enumerate((out_depth, out_first, out_second))
                    for b in range(blocks)
                ]
                for copy in copies:
                    copy.start()
                out_copies += copies

    for d in range(1, flows + 1):

        def sent(c, carry):
            direct(d, c).wait_send()

            @pl.when(relayed(d))
            def _():
                second_leg(d, c).wait_send()

            return carry

        lax.fori_loop(0, SEND_CHUNKS, sent, 0)
    for copy in grid_copies + strip_copies:
        copy.wait_send()
    for copy in out_copies:
        copy.wait()


def body(
    increments, remap_weights, dest_offset, slot_patch, rotation, basis,
    inv_metric_diag, inv_metric_cross, thickness, wind_first, wind_second,
):
    levels, rows, cols = thickness.shape
    lat_rows, top, patch, cells = remap_weights.shape[2:]
    pairs = 3 * levels
    entries = lat_rows * top
    owners, capacity = slot_patch.shape[2:]
    flows = owners - 1
    slots = owners * capacity
    blocks = cols // LANES
    f32 = jnp.float32
    hrows = rows + 2 * EDGE
    packs = -(-3 * rows // GROUPS)
    vmem, dma = pltpu.VMEM, pltpu.SemaphoreType.DMA
    scratch = [
        vmem((W_SLOTS, W_ROWS, top * patch, cells), jnp.bfloat16),
        vmem((pairs, lat_rows, cells), jnp.bfloat16),
        vmem((pairs * W_ROWS, LANES), f32),
        vmem((pairs * W_ROWS, LANES), f32),
        vmem((entries + 1, pairs, LANES), f32),
        vmem((flows, capacity, pairs, LANES), f32),
        vmem((flows, capacity, pairs, LANES), f32),
        vmem((flows, capacity, pairs, LANES), f32),
        vmem((slots + 1, pairs, LANES), f32),
        vmem((3, hrows, blocks + 1, levels, LANES), f32),
        vmem((3, hrows, blocks + 1, levels, LANES), f32),
        vmem((3, hrows, blocks + 1, levels, LANES), f32),
        vmem((4, rows, blocks, levels, LANES), f32),
        vmem((3, blocks, levels, rows, LANES), f32),
        vmem((3, blocks, levels, rows, LANES), f32),
        vmem((3, rows + 16, cols), f32),
        vmem((2, 3, rows + 16, LANES), f32),
        vmem((4, rows, cols), f32),
        vmem((packs, levels, LANES), f32),
        vmem((2, packs + 2, levels, LANES), f32),
        vmem((8, 2 * LANES), jnp.int32),
        vmem((8, LANES), jnp.int32),
        vmem((16, LANES), jnp.int32),
        pltpu.SMEM((16, LANES), jnp.int32),
        dma((W_SLOTS,)),
        dma,
        dma,
        dma((3 + 3 * blocks,)),
        dma((2, 3, blocks)),
        dma((flows, SEND_CHUNKS)),
        dma((flows, SEND_CHUNKS)),
        dma((flows, SEND_CHUNKS)),
        dma((flows, SEND_CHUNKS)),
        dma((8,)),
        dma((8,)),
        dma((8,)),
        dma((8,)),
    ]
    anywhere = pl.BlockSpec(memory_space=pl.ANY)
    on_chip = pl.BlockSpec(memory_space=pltpu.VMEM)
    moved = pl.pallas_call(
        kernel,
        out_shape=[jax.ShapeDtypeStruct(thickness.shape, f32)] * 3,
        in_specs=[on_chip, on_chip, pl.BlockSpec(memory_space=pltpu.SMEM)] + [anywhere] * 8,
        out_specs=[anywhere] * 3,
        scratch_shapes=scratch,
        compiler_params=pltpu.CompilerParams(
            collective_id=0, has_side_effects=True, vmem_limit_bytes=62 * 1024 * 1024
        ),
    )(
        dest_offset[0, 0].T, slot_patch[0, 0], rotation,
        increments.reshape(pairs, lat_rows, cells),
        remap_weights.reshape(lat_rows, top * patch, cells),
        basis, inv_metric_diag, inv_metric_cross, thickness, wind_first, wind_second,
    )
    return tuple(
        pl.pallas_call(
            copy_kernel,
            out_shape=[jax.ShapeDtypeStruct(thickness.shape, f32)] * 3,
            in_specs=[anywhere] * 3,
            out_specs=[anywhere] * 3,
            scratch_shapes=[vmem((3,) + thickness.shape, f32), dma((3,)), dma((3,))],
        )(*moved)
    )


def copy_kernel(depth, first, second, out_depth, out_first, out_second, held, in_sem, out_sem):
    pairs = ((depth, out_depth), (first, out_first), (second, out_second))
    incoming = [pltpu.make_async_copy(src, held.at[i], in_sem.at[i]) for i, (src, _) in enumerate(pairs)]
    outgoing = [pltpu.make_async_copy(held.at[i], dst, out_sem.at[i]) for i, (_, dst) in enumerate(pairs)]
    for copy in incoming:
        copy.start()
    for arrived, copy in zip(incoming, outgoing):
        arrived.wait()
        copy.start()
    for copy in outgoing:
        copy.wait()


def solution(mesh):
    tile = P(None, "ty", "tx")
    in_specs = (
        P(None, None, "tx", "ty"),
        P("tx", "ty", None, None, None, None),
        P("tx", "ty", None, None),
        P("tx", "ty", None, None),
        P(),
        tile,
        tile,
        P("ty", "tx"),
        tile,
        tile,
        tile,
    )
    return jax.shard_map(body, mesh=mesh, in_specs=in_specs, out_specs=(tile, tile, tile), check_vma=False)
```

```python
import jax
import jax.numpy as jnp
from jax import lax
from jax.experimental import pallas as pl
from jax.experimental.pallas import tpu as pltpu
from jax.sharding import PartitionSpec as P

MESH = pl.DeviceIdType.MESH
PANELS = 4
STEPS = 4
HALO = 4
COURANT = 0.15
HALF_GRADIENT = 0.15
FACE_SCALE = 0.5 * COURANT
LANES = 128
GROUPS = 16
NX = 4
SEND_CHUNKS = 6
LAG = 1
EDGE = HALO + 1
ROWS = 4
W_SLOTS = 4
W_ROWS = 16


def kernel(
    offsets, patches, rotation, inc, wts, basis, diag, cross, depth_in, first_in, second_in,
    out_depth, out_first, out_second,
    wbuf, inc_v, half0, half1, term, send, recv, relay, acc, xa, xb, metric, bases,
    state_in, out_v, grid_raw, grid_side, basis_raw, packed, strips, off_v, patch_v, table_v, table,
    w_sem, in_sem, table_sem, field_sem, out_sem, send_sem, recv_sem, relay_send_sem, relay_recv_sem,
    grid_send_sem, grid_recv_sem, halo_send_sem, halo_recv_sem,
):
    tx = lax.axis_index("tx")
    ty = lax.axis_index("ty")
    n_tx = lax.axis_size("tx")
    n_ty = lax.axis_size("ty")
    x = lax.rem(ty, NX)
    odd = lax.rem(tx, 2) == 1
    flows, capacity = send.shape[0], send.shape[1]
    entries = term.shape[0] - 1
    slots = acc.shape[0] - 1
    per = capacity // SEND_CHUNKS
    rows = state_in.shape[3]
    levels = state_in.shape[2]
    blocks = state_in.shape[1]
    w_chunks = wts.shape[0] // W_ROWS

    def dev(dx, dy):
        return (lax.rem(tx + dx + n_tx, n_tx), lax.rem(ty + dy + n_ty, n_ty))

    barrier = pltpu.get_barrier_semaphore()
    partners = [(0, s * d) for d in (1, 2, 3, 4) for s in (1, -1)]
    partners += [(s, d) for s in (1, -1) for d in (-1, 0, 1)]
    for dx, dy in partners:
        pl.semaphore_signal(barrier, inc=1, device_id=dev(dx, dy), device_id_type=MESH)

    def w_copy(chunk, slot):
        return pltpu.make_async_copy(wts.at[pl.ds(chunk * W_ROWS, W_ROWS)], wbuf.at[slot], w_sem.at[slot])

    def inc_copy(chunk, slot):
        return pltpu.make_async_copy(inc.at[:, pl.ds(chunk * W_ROWS, W_ROWS)], inc_v.at[slot], in_sem.at[slot])

    for slot in range(W_SLOTS):
        inc_copy(slot, slot).start()
        w_copy(slot, slot).start()
    field_copies = [
        pltpu.make_async_copy(diag, grid_raw.at[0:2, 8 : 8 + rows], field_sem.at[0]),
        pltpu.make_async_copy(cross, grid_raw.at[2, 8 : 8 + rows], field_sem.at[1]),
        pltpu.make_async_copy(basis, basis_raw, field_sem.at[2]),
    ]
    for i, field in enumerate((depth_in, first_in, second_in)):
        for b in range(blocks):
            field_copies.append(
                pltpu.make_async_copy(
                    field.at[:, :, b * LANES : (b + 1) * LANES], state_in.at[i, b], field_sem.at[3 + i * blocks + b]
                )
            )
    owners = flows + 1
    square = (LANES, LANES)
    row_id = lax.broadcasted_iota(jnp.int32, square, 0)
    col_id = lax.broadcasted_iota(jnp.int32, square, 1)
    tops, lat_rows = offsets.shape
    off_v[...] = jnp.full(off_v.shape, owners, jnp.int32)
    off_v[0:tops, 0:lat_rows] = offsets[...]
    patch_v[...] = jnp.full(patch_v.shape, -1, jnp.int32)
    patch_v[0:owners, 0:capacity] = patches[...]
    off = [off_v[t : t + 1, :] for t in range(tops)]
    wide = off_v.shape[1]
    hits = [[(off[t] == d).astype(jnp.float32) for t in range(tops)] for d in range(owners)]
    stacked = jnp.concatenate([jnp.broadcast_to(hits[d][t], (8, wide)) for d in range(owners) for t in range(tops)], axis=0)
    before_mask = lax.broadcasted_iota(jnp.int32, (wide, wide), 0) < lax.broadcasted_iota(jnp.int32, (wide, wide), 1)
    counts = jnp.dot(
        stacked.astype(jnp.bfloat16), before_mask.astype(jnp.bfloat16), preferred_element_type=jnp.float32
    )
    place = []
    for t in range(tops):
        rank = jnp.zeros((1, wide), jnp.float32)
        for d in range(owners):
            earlier = sum(counts[8 * (d * tops + u) : 8 * (d * tops + u) + 1] for u in range(tops))
            earlier = earlier + sum(hits[d][u] for u in range(t)) if t else earlier
            rank = rank + hits[d][t] * earlier
        place.append(off[t] * LANES + rank.astype(jnp.int32))
    found = [jnp.zeros((1, LANES), jnp.int32) for _ in range(owners)]
    for t in range(tops):
        for h in range(wide // LANES):
            column = jnp.transpose(jnp.broadcast_to(place[t][:, h * LANES : (h + 1) * LANES], square))
            entry = (row_id + h * LANES) * tops + t - entries
            for d in range(owners):
                hit = jnp.where(column == col_id + d * LANES, entry, 0)
                found[d] = found[d] + jnp.sum(hit, axis=0, keepdims=True)
    for d in range(owners):
        table_v[d : d + 1, :] = found[d] + entries

    def order(d, k):
        if d == 0:
            return jnp.where(k < capacity, k, slots)
        chunk = k // per
        return jnp.where(k < capacity, capacity + (chunk * flows + d - 1) * per + (k - chunk * per), slots)

    column_patch = [jnp.transpose(jnp.broadcast_to(patch_v[d : d + 1, :], square)) for d in range(owners)]
    column_order = [order(d, row_id) for d in range(owners)]
    for d in range(owners):
        mine, target = patch_v[d : d + 1, :], order(d, col_id)
        best = jnp.full(square, -1, jnp.int32)
        for e in range(owners):
            hit = jnp.logical_and(column_patch[e] == mine, column_order[e] < target)
            best = jnp.maximum(best, jnp.where(hit, column_order[e], -1))
        best = jnp.max(best, axis=0, keepdims=True)
        table_v[owners + d : owners + d + 1, :] = jnp.where(best < 0, slots, best)
    for h in range(2):
        best = jnp.full(square, -1, jnp.int32)
        for e in range(owners):
            hit = jnp.logical_and(column_patch[e] == col_id + h * LANES, column_order[e] < slots)
            best = jnp.maximum(best, jnp.where(hit, column_order[e], -1))
        best = jnp.max(best, axis=0, keepdims=True)
        table_v[2 * owners + h : 2 * owners + h + 1, :] = jnp.where(best < 0, slots, best)
    table_copy = pltpu.make_async_copy(table_v, table, table_sem)
    table_copy.start()

    zero_row = jnp.zeros(term.shape[1:], jnp.float32)
    term[entries] = zero_row
    acc[slots] = zero_row

    def term_chunk(chunk, carry):
        slot = lax.rem(chunk, W_SLOTS)
        start = chunk * W_ROWS
        inc_copy(chunk, slot).wait()
        cells = inc_v[slot].astype(jnp.float32)
        pairs = cells.shape[0]
        half0[...] = cells[:, :, :LANES].reshape(pairs * W_ROWS, LANES)
        half1[...] = cells[:, :, LANES:].reshape(pairs * W_ROWS, LANES)
        w_copy(chunk, slot).wait()
        for s in range(W_ROWS):
            lhs = jnp.concatenate(
                [half0[pl.ds(s, pairs, stride=W_ROWS), :], half1[pl.ds(s, pairs, stride=W_ROWS), :]], axis=1
            ).astype(jnp.bfloat16)
            product = lax.dot_general(
                lhs, wbuf[slot, s], (((1,), (1,)), ((), ())), preferred_element_type=jnp.float32
            )
            entry = 2 * (start + s)
            term[entry] = product[:, :LANES]
            term[entry + 1] = product[:, LANES:]

        @pl.when(chunk + W_SLOTS < w_chunks)
        def _():
            inc_copy(chunk + W_SLOTS, slot).start()
            w_copy(chunk + W_SLOTS, slot).start()

        return carry

    lax.fori_loop(0, w_chunks, term_chunk, 0)
    for copy in field_copies:
        copy.start()

    table_copy.wait()
    pl.semaphore_wait(barrier, len(partners))

    def direct(d, c):
        part = pl.ds(c * per, per)
        return pltpu.make_async_remote_copy(
            send.at[d - 1, part], recv.at[d - 1, part], send_sem.at[d - 1, c], recv_sem.at[d - 1, c],
            device_id=dev(0, d), device_id_type=MESH,
        )

    def first_leg(d, c):
        part = pl.ds(c * per, per)
        return pltpu.make_async_remote_copy(
            send.at[d - 1, part], relay.at[d - 1, part], send_sem.at[d - 1, c], relay_recv_sem.at[d - 1, c],
            device_id=dev(0, NX), device_id_type=MESH,
        )

    def second_leg(d, c):
        part = pl.ds(c * per, per)
        return pltpu.make_async_remote_copy(
            relay.at[d - 1, part], recv.at[d - 1, part], relay_send_sem.at[d - 1, c], recv_sem.at[d - 1, c],
            device_id=dev(0, d - NX), device_id_type=MESH,
        )

    def relayed(d):
        return jnp.logical_and(odd, x + d >= NX)

    def forward(c):
        for d in range(1, flows + 1):

            @pl.when(relayed(d))
            def _():
                first_leg(d, c).wait_recv()
                second_leg(d, c).start()

    def send_chunk(c, carry):
        for d in range(1, flows + 1):

            def gather(i, inner):
                k = c * per + i
                send[d - 1, k] = term[table[d, k]]
                return inner

            lax.fori_loop(0, per, gather, 0, unroll=6)

            @pl.when(relayed(d))
            def _():
                first_leg(d, c).start()

            @pl.when(jnp.logical_not(relayed(d)))
            def _():
                direct(d, c).start()

        @pl.when(c >= LAG)
        def _():
            forward(c - LAG)

        return carry

    lax.fori_loop(0, SEND_CHUNKS, send_chunk, 0)
    for c in range(SEND_CHUNKS - LAG, SEND_CHUNKS):
        forward(c)

    for copy in field_copies:
        copy.wait()

    own = slice(8, 8 + rows)
    low = slice(8, 16)
    high = slice(rows, 8 + rows)
    below = slice(0, 8)
    above = slice(8 + rows, 16 + rows)
    left = slice(0, LANES)
    right = slice((blocks - 1) * LANES, blocks * LANES)
    grid_moves = [
        (grid_raw.at[:, low], grid_raw.at[:, above], (0, -1)),
        (grid_raw.at[:, high], grid_raw.at[:, below], (0, 1)),
        (grid_raw.at[:, own, left], grid_side.at[0, :, own], (-1, 0)),
        (grid_raw.at[:, low, left], grid_side.at[0, :, above], (-1, -1)),
        (grid_raw.at[:, high, left], grid_side.at[0, :, below], (-1, 1)),
        (grid_raw.at[:, own, right], grid_side.at[1, :, own], (1, 0)),
        (grid_raw.at[:, low, right], grid_side.at[1, :, above], (1, -1)),
        (grid_raw.at[:, high, right], grid_side.at[1, :, below], (1, 1)),
    ]
    grid_copies = [
        pltpu.make_async_remote_copy(
            src, dst, grid_send_sem.at[i], grid_recv_sem.at[i], device_id=dev(*to), device_id_type=MESH
        )
        for i, (src, dst, to) in enumerate(grid_moves)
    ]
    for copy in grid_copies:
        copy.start()

    def accumulate_own(i, carry):
        acc[i] = term[table[0, i]] + acc[table[owners, i]]
        return carry

    lax.fori_loop(0, capacity, accumulate_own, 0, unroll=4)

    shape = (levels, LANES)
    lane = lax.broadcasted_iota(jnp.int32, shape, 1)
    keep_right = jnp.where(tx < n_tx - 1, 1.0, 0.0).astype(jnp.float32)
    keep_left = jnp.where(tx > 0, 1.0, 0.0).astype(jnp.float32)

    def spread(block, j):
        return jnp.broadcast_to(block[j : j + 1], shape)

    def spread_basis(t, carry):
        at = pl.ds(pl.multiple_of(t * 8, 8), 8)
        for k in range(4):
            for b in range(blocks):
                block = basis_raw[k, at, b * LANES : (b + 1) * LANES]
                for j in range(8):
                    bases[k, t * 8 + j, b] = spread(block, j)
        return carry

    lax.fori_loop(0, rows // 8, spread_basis, 0)

    for copy in grid_copies:
        copy.wait_recv()

    def spread_metric(t, carry, picks=range(8)):
        at = pl.ds(pl.multiple_of(t * 8, 8), 8)
        base = t * 8 - 8 + EDGE
        for k in range(3):
            for b in range(blocks):
                block = grid_raw[k, at, b * LANES : (b + 1) * LANES]
                for j in picks:
                    metric[k, base + j, b] = spread(block, j) * FACE_SCALE
            side = jnp.where(lane < LANES // 2, grid_side[0, k, at, :] * (keep_right * FACE_SCALE), grid_side[1, k, at, :] * (keep_left * FACE_SCALE))
            for j in picks:
                metric[k, base + j, blocks] = spread(side, j)
        return carry

    spread_metric(0, 0, range(8 - HALO, 8))
    lax.fori_loop(1, 1 + rows // 8, spread_metric, 0)
    spread_metric(1 + rows // 8, 0, range(HALO))

    def receive_chunk(c, carry):
        for d in range(1, flows + 1):
            direct(d, c).wait_recv()
            base = capacity + (c * flows + d - 1) * per

            def add(i, inner):
                acc[base + i] = recv[d - 1, c * per + i] + acc[table[owners + d, c * per + i]]
                return inner

            lax.fori_loop(0, per, add, 0, unroll=6)
        return carry

    lax.fori_loop(0, SEND_CHUNKS, receive_chunk, 0)

    def regrid(r, carry):
        for b in range(blocks):
            q = r * blocks + b
            patch = acc.at[table[2 * owners + q // LANES, lax.rem(q, LANES)]]
            east, north, thick = patch[0:levels], patch[levels : 2 * levels], patch[2 * levels : 3 * levels]
            at = pl.ds(r, levels, stride=rows)

            def start(i):
                return state_in.at[i, b].reshape(levels * rows, LANES)[at, :]

            xa[0, r + EDGE, b] = start(0) + thick
            xa[1, r + EDGE, b] = start(1) + bases[0, r, b] * east + bases[1, r, b] * north
            xa[2, r + EDGE, b] = start(2) + bases[2, r, b] * east + bases[3, r, b] * north
        return carry

    lax.fori_loop(0, HALO, regrid, 0, unroll=4)
    lax.fori_loop(rows - HALO, rows, regrid, 0, unroll=4)

    def halo_copy(i, src, dst, to):
        return pltpu.make_async_remote_copy(
            src, dst, halo_send_sem.at[i], halo_recv_sem.at[i], device_id=dev(*to), device_id_type=MESH
        )

    row_copies = [
        halo_copy(0, xa.at[:, EDGE : EDGE + HALO, 0:blocks], xa.at[:, EDGE + rows : EDGE + rows + HALO, 0:blocks], (0, -1)),
        halo_copy(1, xa.at[:, EDGE + rows - HALO : EDGE + rows, 0:blocks], xa.at[:, EDGE - HALO : EDGE, 0:blocks], (0, 1)),
    ]
    for copy in row_copies:
        copy.start()

    lax.fori_loop(HALO, rows - HALO, regrid, 0, unroll=4)

    group = lax.rem(lane + HALO, LANES) // (2 * HALO)
    packs = packed.shape[0]
    for v in range(packs):
        total = jnp.zeros(shape, jnp.float32)
        for g in range(GROUPS):
            item = v * GROUPS + g
            f, i = item % 3, item // 3 + EDGE
            edges = jnp.where(lane < LANES // 2, xa[f, i, 0], xa[f, i, blocks - 1])
            moved = pltpu.roll(edges, 2 * HALO * g, 1) if g else edges
            total = jnp.where(group == g, moved, total)
        packed[v] = total

    strip_copies = []
    for side, dx in ((0, -1), (1, 1)):
        strip_copies += [
            halo_copy(2 + 3 * side, packed, strips.at[side, 0:packs], (dx, 0)),
            halo_copy(3 + 3 * side, packed.at[0:1], strips.at[side, packs + 1 : packs + 2], (dx, -1)),
            halo_copy(4 + 3 * side, packed.at[packs - 1 : packs], strips.at[side, packs : packs + 1], (dx, 1)),
        ]
    for copy in strip_copies:
        copy.start()
    for copy in strip_copies:
        copy.wait_recv()

    low_half = lax.rem(lane // HALO, 2) == 0
    halos = [
        jnp.where(low_half, strips[0, v] * keep_right, strips[1, v] * keep_left) for v in range(packs + 2)
    ]
    for r in range(-HALO, rows + HALO):
        for f in range(3):
            item = 3 * (r % rows) + f
            g = item % GROUPS
            v = packs if r < 0 else packs + 1 if r >= rows else item // GROUPS
            xa[f, r + EDGE, blocks] = pltpu.roll(halos[v], LANES - 2 * HALO * g, 1) if g else halos[v]

    ring = blocks + 1
    is_first = lane == 0
    is_last = lane == LANES - 1
    one = jnp.ones(shape, jnp.float32)
    wall_right = jnp.where(is_last, keep_right, one)
    wall_left = jnp.where(is_last, keep_left, one)
    wall_right_halo = jnp.where(is_first, keep_right, one)
    wall_left_tile = jnp.where(is_first, keep_left, one)

    def from_next(values):
        rolled = [pltpu.roll(v, LANES - 1, 1) for v in values]
        return [jnp.where(is_last, rolled[(b + 1) % ring], rolled[b]) for b in range(ring)]

    def from_before(values):
        rolled = [pltpu.roll(v, 1, 1) for v in values]
        return [jnp.where(is_first, rolled[(b - 1) % ring], rolled[b]) for b in range(ring)]

    def load(src, i):
        depth, con_first, con_second = [], [], []
        for b in range(ring):
            first, second = src[1, i, b], src[2, i, b]
            depth.append(src[0, i, b])
            con_first.append(metric[0, i, b] * first + metric[2, i, b] * second)
            con_second.append(metric[2, i, b] * first + metric[1, i, b] * second)
        return depth, con_first, con_second

    def upwind(face, depth_low, depth_high):
        return face * jnp.where(face > 0.0, depth_low, depth_high)

    def row_flux(second_low, second_high, depth_low, depth_high):
        out = []
        for b in range(ring):
            out.append(upwind(second_low[b] + second_high[b], depth_low[b], depth_high[b]))
        return out

    tiles = n_ty // PANELS
    panel = ty // tiles
    place_in_panel = lax.rem(ty, tiles)

    def joint(present, code):
        code = jnp.where(present, code, 0)

        def equals(value):
            return jnp.where(code == value, 1.0, 0.0).astype(jnp.float32)

        return equals(1) - equals(3), equals(0) - equals(2)

    low_joint, high_joint = place_in_panel == 0, place_in_panel == tiles - 1
    low_above = joint(low_joint, rotation[1, lax.rem(panel + PANELS - 1, PANELS)])
    low_below = joint(low_joint, rotation[0, panel])
    high_above = joint(high_joint, rotation[1, panel])
    high_below = joint(high_joint, rotation[0, lax.rem(panel + 1, PANELS)])
    groups = rows // ROWS

    def pick(group, low_turn, high_turn):
        return [
            jnp.where(group == 0, low_turn[k], jnp.where(group == groups, high_turn[k], float(k))) for k in range(2)
        ]

    def turned(turn, con_first, con_second):
        return [turn[0] * con_first[b] + turn[1] * con_second[b] for b in range(ring)]

    def flux_into(src, group):
        i = EDGE - ROWS + group * ROWS
        low, high = load(src, i - 1), load(src, i)
        turn = pick(group - 1, low_below, high_below)
        return row_flux(turned(turn, low[1], low[2]), high[2], low[0], high[0])

    def advance_group(src, store, group, flux_below):
        i = EDGE - ROWS + group * ROWS
        depth_before = [src[0, i - 1, b] for b in range(ring)]
        current = load(src, i)
        for j in range(ROWS):
            depth, con_first, con_second = current
            after = load(src, i + j + 1)
            depth_after, first_after, second_after = after
            if j < ROWS - 1:
                flux_above = row_flux(con_second, second_after, depth, depth_after)
                flux_next = flux_above
            else:
                turn_above = pick(group, low_above, high_above)
                turn_below = pick(group, low_below, high_below)
                flux_above = row_flux(con_second, turned(turn_above, first_after, second_after), depth, depth_after)
                flux_next = row_flux(turned(turn_below, con_first, con_second), second_after, depth, depth_after)
            depth_right, first_right = from_next(depth), from_next(con_first)
            depth_left, first_left = from_before(depth), from_before(con_first)
            for b in range(ring):
                face = con_first[b] + first_right[b]
                if b == blocks - 1:
                    face = face * wall_right
                if b == blocks:
                    face = face * wall_left
                flux_right = upwind(face, depth[b], depth_right[b])
                face = con_first[b] + first_left[b]
                if b == blocks:
                    face = face * wall_right_halo
                if b == 0:
                    face = face * wall_left_tile
                flux_left = upwind(face, depth_left[b], depth[b])
                new_depth = depth[b] - ((flux_right - flux_left) + (flux_above[b] - flux_below[b]))
                new_first = src[1, i + j, b] - HALF_GRADIENT * (depth_right[b] - depth_left[b])
                new_second = src[2, i + j, b] - HALF_GRADIENT * (depth_after[b] - depth_before[b])
                store(i + j, b, (new_depth, new_first, new_second))
            depth_before, current, flux_below = depth, after, flux_next
        return flux_below

    for step in range(STEPS):
        src, dst = (xa, xb) if step % 2 == 0 else (xb, xa)

        def store_state(i, b, values, dst=dst):
            for f in range(3):
                dst[f, i, b] = values[f]

        def store_out(i, b, values):
            if b < blocks:
                for f in range(3):
                    out_v.at[f, b].reshape(levels * rows, LANES)[pl.ds(i - EDGE, levels, stride=rows), :] = values[f]

        store = store_out if step == STEPS - 1 else store_state

        def sweep(first, end, src=src, store=store):
            lax.fori_loop(
                first, end, lambda g, flux: tuple(advance_group(src, store, g, flux)), tuple(flux_into(src, first)),
                unroll=2,
            )

        if step == 0:
            sweep(2, groups)
            for copy in row_copies:
                copy.wait_recv()
            sweep(0, 2)
            sweep(groups, groups + 2)
            for copy in row_copies:
                copy.wait_send()
        elif step < STEPS - 1:
            sweep(0, groups + 2)
        else:
            out_copies = []
            half = rows // 2
            for part in range(2):
                sweep(1 + part * groups // 2, 1 + (part + 1) * groups // 2)
                span = slice(part * half, (part + 1) * half)
                copies = [
                    pltpu.make_async_copy(
                        out_v.at[f, b, :, span], out.at[:, span, b * LANES : (b + 1) * LANES], out_sem.at[part, f, b]
                    )
                    for f, out in enumerate((out_depth, out_first, out_second))
                    for b in range(blocks)
                ]
                for copy in copies:
                    copy.start()
                out_copies += copies

    for d in range(1, flows + 1):

        def sent(c, carry):
            direct(d, c).wait_send()

            @pl.when(relayed(d))
            def _():
                second_leg(d, c).wait_send()

            return carry

        lax.fori_loop(0, SEND_CHUNKS, sent, 0)
    for copy in grid_copies + strip_copies:
        copy.wait_send()
    for copy in out_copies:
        copy.wait()


def body(
    increments, remap_weights, dest_offset, slot_patch, rotation, basis,
    inv_metric_diag, inv_metric_cross, thickness, wind_first, wind_second,
):
    levels, rows, cols = thickness.shape
    lat_rows, top, patch, cells = remap_weights.shape[2:]
    pairs = 3 * levels
    entries = lat_rows * top
    owners, capacity = slot_patch.shape[2:]
    flows = owners - 1
    slots = owners * capacity
    blocks = cols // LANES
    f32 = jnp.float32
    hrows = rows + 2 * EDGE
    packs = -(-3 * rows // GROUPS)
    vmem, dma = pltpu.VMEM, pltpu.SemaphoreType.DMA
    scratch = [
        vmem((W_SLOTS, W_ROWS, top * patch, cells), jnp.bfloat16),
        vmem((W_SLOTS, pairs, W_ROWS, cells), jnp.bfloat16),
        vmem((pairs * W_ROWS, LANES), f32),
        vmem((pairs * W_ROWS, LANES), f32),
        vmem((entries + 1, pairs, LANES), f32),
        vmem((flows, capacity, pairs, LANES), f32),
        vmem((flows, capacity, pairs, LANES), f32),
        vmem((flows, capacity, pairs, LANES), f32),
        vmem((slots + 1, pairs, LANES), f32),
        vmem((3, hrows, blocks + 1, levels, LANES), f32),
        vmem((3, hrows, blocks + 1, levels, LANES), f32),
        vmem((3, hrows, blocks + 1, levels, LANES), f32),
        vmem((4, rows, blocks, levels, LANES), f32),
        vmem((3, blocks, levels, rows, LANES), f32),
        vmem((3, blocks, levels, rows, LANES), f32),
        vmem((3, rows + 16, cols), f32),
        vmem((2, 3, rows + 16, LANES), f32),
        vmem((4, rows, cols), f32),
        vmem((packs, levels, LANES), f32),
        vmem((2, packs + 2, levels, LANES), f32),
        vmem((8, 2 * LANES), jnp.int32),
        vmem((8, LANES), jnp.int32),
        vmem((16, LANES), jnp.int32),
        pltpu.SMEM((16, LANES), jnp.int32),
        dma((W_SLOTS,)),
        dma((W_SLOTS,)),
        dma,
        dma((3 + 3 * blocks,)),
        dma((2, 3, blocks)),
        dma((flows, SEND_CHUNKS)),
        dma((flows, SEND_CHUNKS)),
        dma((flows, SEND_CHUNKS)),
        dma((flows, SEND_CHUNKS)),
        dma((8,)),
        dma((8,)),
        dma((8,)),
        dma((8,)),
    ]
    anywhere = pl.BlockSpec(memory_space=pl.ANY)
    on_chip = pl.BlockSpec(memory_space=pltpu.VMEM)
    moved = pl.pallas_call(
        kernel,
        out_shape=[jax.ShapeDtypeStruct(thickness.shape, f32)] * 3,
        in_specs=[on_chip, on_chip, pl.BlockSpec(memory_space=pltpu.SMEM)] + [anywhere] * 8,
        out_specs=[anywhere] * 3,
        scratch_shapes=scratch,
        compiler_params=pltpu.CompilerParams(
            collective_id=0, has_side_effects=True, vmem_limit_bytes=62 * 1024 * 1024
        ),
    )(
        dest_offset[0, 0].T, slot_patch[0, 0], rotation,
        increments.reshape(pairs, lat_rows, cells),
        remap_weights.reshape(lat_rows, top * patch, cells),
        basis, inv_metric_diag, inv_metric_cross, thickness, wind_first, wind_second,
    )
    return tuple(
        pl.pallas_call(
            copy_kernel,
            out_shape=[jax.ShapeDtypeStruct(thickness.shape, f32)] * 3,
            in_specs=[anywhere] * 3,
            out_specs=[anywhere] * 3,
            scratch_shapes=[vmem((3,) + thickness.shape, f32), dma((3,)), dma((3,))],
        )(*moved)
    )


def copy_kernel(depth, first, second, out_depth, out_first, out_second, held, in_sem, out_sem):
    pairs = ((depth, out_depth), (first, out_first), (second, out_second))
    incoming = [pltpu.make_async_copy(src, held.at[i], in_sem.at[i]) for i, (src, _) in enumerate(pairs)]
    outgoing = [pltpu.make_async_copy(held.at[i], dst, out_sem.at[i]) for i, (_, dst) in enumerate(pairs)]
    for copy in incoming:
        copy.start()
    for arrived, copy in zip(incoming, outgoing):
        arrived.wait()
        copy.start()
    for copy in outgoing:
        copy.wait()


def solution(mesh):
    tile = P(None, "ty", "tx")
    in_specs = (
        P(None, None, "tx", "ty"),
        P("tx", "ty", None, None, None, None),
        P("tx", "ty", None, None),
        P("tx", "ty", None, None),
        P(),
        tile,
        tile,
        P("ty", "tx"),
        tile,
        tile,
        tile,
    )
    return jax.shard_map(body, mesh=mesh, in_specs=in_specs, out_specs=(tile, tile, tile), check_vma=False)
```

```python
import jax
import jax.numpy as jnp
from jax import lax
from jax.experimental import pallas as pl
from jax.experimental.pallas import tpu as pltpu
from jax.sharding import PartitionSpec as P

MESH = pl.DeviceIdType.MESH
PANELS = 4
STEPS = 4
HALO = 4
COURANT = 0.15
HALF_GRADIENT = 0.15
FACE_SCALE = 0.5 * COURANT
LANES = 128
GROUPS = 16
NX = 4
SEND_CHUNKS = 6
LAG = 1
EDGE = HALO + 1
ROWS = 4
W_SLOTS = 4
W_ROWS = 16


def kernel(
    offsets, patches, rotation, inc, wts, basis, diag, cross, depth_in, first_in, second_in,
    out_depth, out_first, out_second,
    wbuf, inc_v, half0, half1, term, send, recv, relay, acc, xa, xb, metric, bases,
    state_in, out_v, grid_raw, grid_side, basis_raw, packed, strips, off_v, patch_v, table_v, table,
    w_sem, in_sem, table_sem, field_sem, out_sem, send_sem, recv_sem, relay_send_sem, relay_recv_sem,
    grid_send_sem, grid_recv_sem, halo_send_sem, halo_recv_sem,
):
    tx = lax.axis_index("tx")
    ty = lax.axis_index("ty")
    n_tx = lax.axis_size("tx")
    n_ty = lax.axis_size("ty")
    x = lax.rem(ty, NX)
    odd = lax.rem(tx, 2) == 1
    flows, capacity = send.shape[0], send.shape[1]
    entries = term.shape[0] - 1
    slots = acc.shape[0] - 1
    per = capacity // SEND_CHUNKS
    rows = state_in.shape[3]
    levels = state_in.shape[2]
    blocks = state_in.shape[1]
    w_chunks = wts.shape[0] // W_ROWS

    def dev(dx, dy):
        return (lax.rem(tx + dx + n_tx, n_tx), lax.rem(ty + dy + n_ty, n_ty))

    barrier = pltpu.get_barrier_semaphore()
    partners = [(0, s * d) for d in (1, 2, 3, 4) for s in (1, -1)]
    partners += [(s, d) for s in (1, -1) for d in (-1, 0, 1)]
    for dx, dy in partners:
        pl.semaphore_signal(barrier, inc=1, device_id=dev(dx, dy), device_id_type=MESH)

    def w_copy(chunk, slot):
        return pltpu.make_async_copy(wts.at[pl.ds(chunk * W_ROWS, W_ROWS)], wbuf.at[slot], w_sem.at[slot])

    def inc_copy(chunk, slot):
        return pltpu.make_async_copy(inc.at[:, pl.ds(chunk * W_ROWS, W_ROWS)], inc_v.at[slot], in_sem.at[slot])

    for slot in range(W_SLOTS):
        inc_copy(slot, slot).start()
        w_copy(slot, slot).start()
    field_copies = [
        pltpu.make_async_copy(diag, grid_raw.at[0:2, 8 : 8 + rows], field_sem.at[0]),
        pltpu.make_async_copy(cross, grid_raw.at[2, 8 : 8 + rows], field_sem.at[1]),
        pltpu.make_async_copy(basis, basis_raw, field_sem.at[2]),
    ]
    for i, field in enumerate((depth_in, first_in, second_in)):
        for b in range(blocks):
            field_copies.append(
                pltpu.make_async_copy(
                    field.at[:, :, b * LANES : (b + 1) * LANES], state_in.at[i, b], field_sem.at[3 + i * blocks + b]
                )
            )
    owners = flows + 1
    square = (LANES, LANES)
    row_id = lax.broadcasted_iota(jnp.int32, square, 0)
    col_id = lax.broadcasted_iota(jnp.int32, square, 1)
    tops, lat_rows = offsets.shape
    off_v[...] = jnp.full(off_v.shape, owners, jnp.int32)
    off_v[0:tops, 0:lat_rows] = offsets[...]
    patch_v[...] = jnp.full(patch_v.shape, -1, jnp.int32)
    patch_v[0:owners, 0:capacity] = patches[...]
    off = [off_v[t : t + 1, :] for t in range(tops)]
    wide = off_v.shape[1]
    hits = [[(off[t] == d).astype(jnp.float32) for t in range(tops)] for d in range(owners)]
    stacked = jnp.concatenate([jnp.broadcast_to(hits[d][t], (8, wide)) for d in range(owners) for t in range(tops)], axis=0)
    before_mask = lax.broadcasted_iota(jnp.int32, (wide, wide), 0) < lax.broadcasted_iota(jnp.int32, (wide, wide), 1)
    counts = jnp.dot(
        stacked.astype(jnp.bfloat16), before_mask.astype(jnp.bfloat16), preferred_element_type=jnp.float32
    )
    place = []
    for t in range(tops):
        rank = jnp.zeros((1, wide), jnp.float32)
        for d in range(owners):
            earlier = sum(counts[8 * (d * tops + u) : 8 * (d * tops + u) + 1] for u in range(tops))
            earlier = earlier + sum(hits[d][u] for u in range(t)) if t else earlier
            rank = rank + hits[d][t] * earlier
        place.append(off[t] * LANES + rank.astype(jnp.int32))
    found = [jnp.zeros((1, LANES), jnp.int32) for _ in range(owners)]
    for t in range(tops):
        for h in range(wide // LANES):
            column = jnp.transpose(jnp.broadcast_to(place[t][:, h * LANES : (h + 1) * LANES], square))
            entry = (row_id + h * LANES) * tops + t - entries
            for d in range(owners):
                hit = jnp.where(column == col_id + d * LANES, entry, 0)
                found[d] = found[d] + jnp.sum(hit, axis=0, keepdims=True)
    for d in range(owners):
        table_v[d : d + 1, :] = found[d] + entries

    def order(d, k):
        if d == 0:
            return jnp.where(k < capacity, k, slots)
        chunk = k // per
        return jnp.where(k < capacity, capacity + (chunk * flows + d - 1) * per + (k - chunk * per), slots)

    column_patch = [jnp.transpose(jnp.broadcast_to(patch_v[d : d + 1, :], square)) for d in range(owners)]
    column_order = [order(d, row_id) for d in range(owners)]
    for d in range(owners):
        mine, target = patch_v[d : d + 1, :], order(d, col_id)
        best = jnp.full(square, -1, jnp.int32)
        for e in range(owners):
            hit = jnp.logical_and(column_patch[e] == mine, column_order[e] < target)
            best = jnp.maximum(best, jnp.where(hit, column_order[e], -1))
        best = jnp.max(best, axis=0, keepdims=True)
        table_v[owners + d : owners + d + 1, :] = jnp.where(best < 0, slots, best)
    for h in range(2):
        best = jnp.full(square, -1, jnp.int32)
        for e in range(owners):
            hit = jnp.logical_and(column_patch[e] == col_id + h * LANES, column_order[e] < slots)
            best = jnp.maximum(best, jnp.where(hit, column_order[e], -1))
        best = jnp.max(best, axis=0, keepdims=True)
        table_v[2 * owners + h : 2 * owners + h + 1, :] = jnp.where(best < 0, slots, best)
    table_copy = pltpu.make_async_copy(table_v, table, table_sem)
    table_copy.start()

    zero_row = jnp.zeros(term.shape[1:], jnp.float32)
    term[entries] = zero_row
    acc[slots] = zero_row

    def term_chunk(chunk, carry):
        slot = lax.rem(chunk, W_SLOTS)
        start = chunk * W_ROWS
        inc_copy(chunk, slot).wait()
        cells = inc_v[slot].astype(jnp.float32)
        pairs = cells.shape[0]
        half0[...] = cells[:, :, :LANES].reshape(pairs * W_ROWS, LANES)
        half1[...] = cells[:, :, LANES:].reshape(pairs * W_ROWS, LANES)
        w_copy(chunk, slot).wait()
        for s in range(W_ROWS):
            lhs = jnp.concatenate(
                [half0[pl.ds(s, pairs, stride=W_ROWS), :], half1[pl.ds(s, pairs, stride=W_ROWS), :]], axis=1
            ).astype(jnp.bfloat16)
            product = lax.dot_general(
                lhs, wbuf[slot, s], (((1,), (1,)), ((), ())), preferred_element_type=jnp.float32
            )
            entry = 2 * (start + s)
            term[entry] = product[:, :LANES]
            term[entry + 1] = product[:, LANES:]

        @pl.when(chunk + W_SLOTS < w_chunks)
        def _():
            inc_copy(chunk + W_SLOTS, slot).start()
            w_copy(chunk + W_SLOTS, slot).start()

        return carry

    lax.fori_loop(0, w_chunks, term_chunk, 0)
    for copy in field_copies:
        copy.start()

    table_copy.wait()
    pl.semaphore_wait(barrier, len(partners))

    def direct(d, c):
        part = pl.ds(c * per, per)
        return pltpu.make_async_remote_copy(
            send.at[d - 1, part], recv.at[d - 1, part], send_sem.at[d - 1, c], recv_sem.at[d - 1, c],
            device_id=dev(0, d), device_id_type=MESH,
        )

    def first_leg(d, c):
        part = pl.ds(c * per, per)
        return pltpu.make_async_remote_copy(
            send.at[d - 1, part], relay.at[d - 1, part], send_sem.at[d - 1, c], relay_recv_sem.at[d - 1, c],
            device_id=dev(0, NX), device_id_type=MESH,
        )

    def second_leg(d, c):
        part = pl.ds(c * per, per)
        return pltpu.make_async_remote_copy(
            relay.at[d - 1, part], recv.at[d - 1, part], relay_send_sem.at[d - 1, c], recv_sem.at[d - 1, c],
            device_id=dev(0, d - NX), device_id_type=MESH,
        )

    def relayed(d):
        return jnp.logical_and(odd, x + d >= NX)

    def forward(c):
        for d in range(1, flows + 1):

            @pl.when(relayed(d))
            def _():
                first_leg(d, c).wait_recv()
                second_leg(d, c).start()

    def send_chunk(c, carry):
        for d in range(1, flows + 1):

            def gather(i, inner):
                k = c * per + i
                send[d - 1, k] = term[table[d, k]]
                return inner

            lax.fori_loop(0, per, gather, 0, unroll=6)

            @pl.when(relayed(d))
            def _():
                first_leg(d, c).start()

            @pl.when(jnp.logical_not(relayed(d)))
            def _():
                direct(d, c).start()

        @pl.when(c >= LAG)
        def _():
            forward(c - LAG)

        return carry

    lax.fori_loop(0, SEND_CHUNKS, send_chunk, 0)
    for c in range(SEND_CHUNKS - LAG, SEND_CHUNKS):
        forward(c)

    for copy in field_copies:
        copy.wait()

    own = slice(8, 8 + rows)
    low = slice(8, 16)
    high = slice(rows, 8 + rows)
    below = slice(0, 8)
    above = slice(8 + rows, 16 + rows)
    left = slice(0, LANES)
    right = slice((blocks - 1) * LANES, blocks * LANES)
    grid_moves = [
        (grid_raw.at[:, low], grid_raw.at[:, above], (0, -1)),
        (grid_raw.at[:, high], grid_raw.at[:, below], (0, 1)),
        (grid_raw.at[:, own, left], grid_side.at[0, :, own], (-1, 0)),
        (grid_raw.at[:, low, left], grid_side.at[0, :, above], (-1, -1)),
        (grid_raw.at[:, high, left], grid_side.at[0, :, below], (-1, 1)),
        (grid_raw.at[:, own, right], grid_side.at[1, :, own], (1, 0)),
        (grid_raw.at[:, low, right], grid_side.at[1, :, above], (1, -1)),
        (grid_raw.at[:, high, right], grid_side.at[1, :, below], (1, 1)),
    ]
    grid_copies = [
        pltpu.make_async_remote_copy(
            src, dst, grid_send_sem.at[i], grid_recv_sem.at[i], device_id=dev(*to), device_id_type=MESH
        )
        for i, (src, dst, to) in enumerate(grid_moves)
    ]
    for copy in grid_copies:
        copy.start()

    def accumulate_own(i, carry):
        acc[i] = term[table[0, i]] + acc[table[owners, i]]
        return carry

    lax.fori_loop(0, capacity, accumulate_own, 0, unroll=4)

    shape = (levels, LANES)
    lane = lax.broadcasted_iota(jnp.int32, shape, 1)
    keep_right = jnp.where(tx < n_tx - 1, 1.0, 0.0).astype(jnp.float32)
    keep_left = jnp.where(tx > 0, 1.0, 0.0).astype(jnp.float32)

    def spread(block, j):
        return jnp.broadcast_to(block[j : j + 1], shape)

    def spread_basis(t, carry):
        at = pl.ds(pl.multiple_of(t * 8, 8), 8)
        for k in range(4):
            for b in range(blocks):
                block = basis_raw[k, at, b * LANES : (b + 1) * LANES]
                for j in range(8):
                    bases[k, t * 8 + j, b] = spread(block, j)
        return carry

    lax.fori_loop(0, rows // 8, spread_basis, 0)

    for copy in grid_copies:
        copy.wait_recv()

    def spread_metric(t, carry, picks=range(8)):
        at = pl.ds(pl.multiple_of(t * 8, 8), 8)
        base = t * 8 - 8 + EDGE
        for k in range(3):
            for b in range(blocks):
                block = grid_raw[k, at, b * LANES : (b + 1) * LANES]
                for j in picks:
                    metric[k, base + j, b] = spread(block, j) * FACE_SCALE
            side = jnp.where(lane < LANES // 2, grid_side[0, k, at, :] * (keep_right * FACE_SCALE), grid_side[1, k, at, :] * (keep_left * FACE_SCALE))
            for j in picks:
                metric[k, base + j, blocks] = spread(side, j)
        return carry

    spread_metric(0, 0, range(8 - HALO, 8))
    lax.fori_loop(1, 1 + rows // 8, spread_metric, 0)
    spread_metric(1 + rows // 8, 0, range(HALO))

    def receive_chunk(c, carry):
        for d in range(1, flows + 1):
            direct(d, c).wait_recv()
            base = capacity + (c * flows + d - 1) * per

            def add(i, inner):
                acc[base + i] = recv[d - 1, c * per + i] + acc[table[owners + d, c * per + i]]
                return inner

            lax.fori_loop(0, per, add, 0, unroll=per)
        return carry

    lax.fori_loop(0, SEND_CHUNKS, receive_chunk, 0)

    def regrid(r, carry):
        for b in range(blocks):
            q = r * blocks + b
            patch = acc.at[table[2 * owners + q // LANES, lax.rem(q, LANES)]]
            east, north, thick = patch[0:levels], patch[levels : 2 * levels], patch[2 * levels : 3 * levels]
            at = pl.ds(r, levels, stride=rows)

            def start(i):
                return state_in.at[i, b].reshape(levels * rows, LANES)[at, :]

            xa[0, r + EDGE, b] = start(0) + thick
            xa[1, r + EDGE, b] = start(1) + bases[0, r, b] * east + bases[1, r, b] * north
            xa[2, r + EDGE, b] = start(2) + bases[2, r, b] * east + bases[3, r, b] * north
        return carry

    lax.fori_loop(0, HALO, regrid, 0, unroll=4)
    lax.fori_loop(rows - HALO, rows, regrid, 0, unroll=4)

    def halo_copy(i, src, dst, to):
        return pltpu.make_async_remote_copy(
            src, dst, halo_send_sem.at[i], halo_recv_sem.at[i], device_id=dev(*to), device_id_type=MESH
        )

    row_copies = [
        halo_copy(0, xa.at[:, EDGE : EDGE + HALO, 0:blocks], xa.at[:, EDGE + rows : EDGE + rows + HALO, 0:blocks], (0, -1)),
        halo_copy(1, xa.at[:, EDGE + rows - HALO : EDGE + rows, 0:blocks], xa.at[:, EDGE - HALO : EDGE, 0:blocks], (0, 1)),
    ]
    for copy in row_copies:
        copy.start()

    lax.fori_loop(HALO, rows - HALO, regrid, 0, unroll=4)

    group = lax.rem(lane + HALO, LANES) // (2 * HALO)
    packs = packed.shape[0]
    for v in range(packs):
        total = jnp.zeros(shape, jnp.float32)
        for g in range(GROUPS):
            item = v * GROUPS + g
            f, i = item % 3, item // 3 + EDGE
            edges = jnp.where(lane < LANES // 2, xa[f, i, 0], xa[f, i, blocks - 1])
            moved = pltpu.roll(edges, 2 * HALO * g, 1) if g else edges
            total = jnp.where(group == g, moved, total)
        packed[v] = total

    strip_copies = []
    for side, dx in ((0, -1), (1, 1)):
        strip_copies += [
            halo_copy(2 + 3 * side, packed, strips.at[side, 0:packs], (dx, 0)),
            halo_copy(3 + 3 * side, packed.at[0:1], strips.at[side, packs + 1 : packs + 2], (dx, -1)),
            halo_copy(4 + 3 * side, packed.at[packs - 1 : packs], strips.at[side, packs : packs + 1], (dx, 1)),
        ]
    for copy in strip_copies:
        copy.start()
    for copy in strip_copies:
        copy.wait_recv()

    low_half = lax.rem(lane // HALO, 2) == 0
    halos = [
        jnp.where(low_half, strips[0, v] * keep_right, strips[1, v] * keep_left) for v in range(packs + 2)
    ]
    for r in range(-HALO, rows + HALO):
        for f in range(3):
            item = 3 * (r % rows) + f
            g = item % GROUPS
            v = packs if r < 0 else packs + 1 if r >= rows else item // GROUPS
            xa[f, r + EDGE, blocks] = pltpu.roll(halos[v], LANES - 2 * HALO * g, 1) if g else halos[v]

    ring = blocks + 1
    is_first = lane == 0
    is_last = lane == LANES - 1
    one = jnp.ones(shape, jnp.float32)
    wall_right = jnp.where(is_last, keep_right, one)
    wall_left = jnp.where(is_last, keep_left, one)
    wall_right_halo = jnp.where(is_first, keep_right, one)
    wall_left_tile = jnp.where(is_first, keep_left, one)

    def from_next(values):
        rolled = [pltpu.roll(v, LANES - 1, 1) for v in values]
        return [jnp.where(is_last, rolled[(b + 1) % ring], rolled[b]) for b in range(ring)]

    def from_before(values):
        rolled = [pltpu.roll(v, 1, 1) for v in values]
        return [jnp.where(is_first, rolled[(b - 1) % ring], rolled[b]) for b in range(ring)]

    def load(src, i):
        depth, con_first, con_second = [], [], []
        for b in range(ring):
            first, second = src[1, i, b], src[2, i, b]
            depth.append(src[0, i, b])
            con_first.append(metric[0, i, b] * first + metric[2, i, b] * second)
            con_second.append(metric[2, i, b] * first + metric[1, i, b] * second)
        return depth, con_first, con_second

    def upwind(face, depth_low, depth_high):
        return face * jnp.where(face > 0.0, depth_low, depth_high)

    def row_flux(second_low, second_high, depth_low, depth_high):
        out = []
        for b in range(ring):
            out.append(upwind(second_low[b] + second_high[b], depth_low[b], depth_high[b]))
        return out

    tiles = n_ty // PANELS
    panel = ty // tiles
    place_in_panel = lax.rem(ty, tiles)

    def joint(present, code):
        code = jnp.where(present, code, 0)

        def equals(value):
            return jnp.where(code == value, 1.0, 0.0).astype(jnp.float32)

        return equals(1) - equals(3), equals(0) - equals(2)

    low_joint, high_joint = place_in_panel == 0, place_in_panel == tiles - 1
    low_above = joint(low_joint, rotation[1, lax.rem(panel + PANELS - 1, PANELS)])
    low_below = joint(low_joint, rotation[0, panel])
    high_above = joint(high_joint, rotation[1, panel])
    high_below = joint(high_joint, rotation[0, lax.rem(panel + 1, PANELS)])
    groups = rows // ROWS

    def pick(group, low_turn, high_turn):
        return [
            jnp.where(group == 0, low_turn[k], jnp.where(group == groups, high_turn[k], float(k))) for k in range(2)
        ]

    def turned(turn, con_first, con_second):
        return [turn[0] * con_first[b] + turn[1] * con_second[b] for b in range(ring)]

    def flux_into(src, group):
        i = EDGE - ROWS + group * ROWS
        low, high = load(src, i - 1), load(src, i)
        turn = pick(group - 1, low_below, high_below)
        return row_flux(turned(turn, low[1], low[2]), high[2], low[0], high[0])

    def advance_group(src, store, group, flux_below):
        i = EDGE - ROWS + group * ROWS
        depth_before = [src[0, i - 1, b] for b in range(ring)]
        current = load(src, i)
        for j in range(ROWS):
            depth, con_first, con_second = current
            after = load(src, i + j + 1)
            depth_after, first_after, second_after = after
            if j < ROWS - 1:
                flux_above = row_flux(con_second, second_after, depth, depth_after)
                flux_next = flux_above
            else:
                turn_above = pick(group, low_above, high_above)
                turn_below = pick(group, low_below, high_below)
                flux_above = row_flux(con_second, turned(turn_above, first_after, second_after), depth, depth_after)
                flux_next = row_flux(turned(turn_below, con_first, con_second), second_after, depth, depth_after)
            depth_right, first_right = from_next(depth), from_next(con_first)
            depth_left, first_left = from_before(depth), from_before(con_first)
            for b in range(ring):
                face = con_first[b] + first_right[b]
                if b == blocks - 1:
                    face = face * wall_right
                if b == blocks:
                    face = face * wall_left
                flux_right = upwind(face, depth[b], depth_right[b])
                face = con_first[b] + first_left[b]
                if b == blocks:
                    face = face * wall_right_halo
                if b == 0:
                    face = face * wall_left_tile
                flux_left = upwind(face, depth_left[b], depth[b])
                new_depth = depth[b] - ((flux_right - flux_left) + (flux_above[b] - flux_below[b]))
                new_first = src[1, i + j, b] - HALF_GRADIENT * (depth_right[b] - depth_left[b])
                new_second = src[2, i + j, b] - HALF_GRADIENT * (depth_after[b] - depth_before[b])
                store(i + j, b, (new_depth, new_first, new_second))
            depth_before, current, flux_below = depth, after, flux_next
        return flux_below

    for step in range(STEPS):
        src, dst = (xa, xb) if step % 2 == 0 else (xb, xa)

        def store_state(i, b, values, dst=dst):
            for f in range(3):
                dst[f, i, b] = values[f]

        def store_out(i, b, values):
            if b < blocks:
                for f in range(3):
                    out_v.at[f, b].reshape(levels * rows, LANES)[pl.ds(i - EDGE, levels, stride=rows), :] = values[f]

        store = store_out if step == STEPS - 1 else store_state

        def sweep(first, end, src=src, store=store):
            lax.fori_loop(
                first, end, lambda g, flux: tuple(advance_group(src, store, g, flux)), tuple(flux_into(src, first)),
                unroll=max(2, (end - first) // 2),
            )

        if step == 0:
            sweep(2, groups)
            for copy in row_copies:
                copy.wait_recv()
            sweep(0, 2)
            sweep(groups, groups + 2)
            for copy in row_copies:
                copy.wait_send()
        elif step < STEPS - 1:
            sweep(0, groups + 2)
        else:
            out_copies = []
            half = rows // 2
            for part in range(2):
                sweep(1 + part * groups // 2, 1 + (part + 1) * groups // 2)
                span = slice(part * half, (part + 1) * half)
                copies = [
                    pltpu.make_async_copy(
                        out_v.at[f, b, :, span], out.at[:, span, b * LANES : (b + 1) * LANES], out_sem.at[part, f, b]
                    )
                    for f, out in enumerate((out_depth, out_first, out_second))
                    for b in range(blocks)
                ]
                for copy in copies:
                    copy.start()
                out_copies += copies

    for d in range(1, flows + 1):

        def sent(c, carry):
            direct(d, c).wait_send()

            @pl.when(relayed(d))
            def _():
                second_leg(d, c).wait_send()

            return carry

        lax.fori_loop(0, SEND_CHUNKS, sent, 0)
    for copy in grid_copies + strip_copies:
        copy.wait_send()
    for copy in out_copies:
        copy.wait()


def body(
    increments, remap_weights, dest_offset, slot_patch, rotation, basis,
    inv_metric_diag, inv_metric_cross, thickness, wind_first, wind_second,
):
    levels, rows, cols = thickness.shape
    lat_rows, top, patch, cells = remap_weights.shape[2:]
    pairs = 3 * levels
    entries = lat_rows * top
    owners, capacity = slot_patch.shape[2:]
    flows = owners - 1
    slots = owners * capacity
    blocks = cols // LANES
    f32 = jnp.float32
    hrows = rows + 2 * EDGE
    packs = -(-3 * rows // GROUPS)
    vmem, dma = pltpu.VMEM, pltpu.SemaphoreType.DMA
    scratch = [
        vmem((W_SLOTS, W_ROWS, top * patch, cells), jnp.bfloat16),
        vmem((W_SLOTS, pairs, W_ROWS, cells), jnp.bfloat16),
        vmem((pairs * W_ROWS, LANES), f32),
        vmem((pairs * W_ROWS, LANES), f32),
        vmem((entries + 1, pairs, LANES), f32),
        vmem((flows, capacity, pairs, LANES), f32),
        vmem((flows, capacity, pairs, LANES), f32),
        vmem((flows, capacity, pairs, LANES), f32),
        vmem((slots + 1, pairs, LANES), f32),
        vmem((3, hrows, blocks + 1, levels, LANES), f32),
        vmem((3, hrows, blocks + 1, levels, LANES), f32),
        vmem((3, hrows, blocks + 1, levels, LANES), f32),
        vmem((4, rows, blocks, levels, LANES), f32),
        vmem((3, blocks, levels, rows, LANES), f32),
        vmem((3, blocks, levels, rows, LANES), f32),
        vmem((3, rows + 16, cols), f32),
        vmem((2, 3, rows + 16, LANES), f32),
        vmem((4, rows, cols), f32),
        vmem((packs, levels, LANES), f32),
        vmem((2, packs + 2, levels, LANES), f32),
        vmem((8, 2 * LANES), jnp.int32),
        vmem((8, LANES), jnp.int32),
        vmem((16, LANES), jnp.int32),
        pltpu.SMEM((16, LANES), jnp.int32),
        dma((W_SLOTS,)),
        dma((W_SLOTS,)),
        dma,
        dma((3 + 3 * blocks,)),
        dma((2, 3, blocks)),
        dma((flows, SEND_CHUNKS)),
        dma((flows, SEND_CHUNKS)),
        dma((flows, SEND_CHUNKS)),
        dma((flows, SEND_CHUNKS)),
        dma((8,)),
        dma((8,)),
        dma((8,)),
        dma((8,)),
    ]
    anywhere = pl.BlockSpec(memory_space=pl.ANY)
    on_chip = pl.BlockSpec(memory_space=pltpu.VMEM)
    moved = pl.pallas_call(
        kernel,
        out_shape=[jax.ShapeDtypeStruct(thickness.shape, f32)] * 3,
        in_specs=[on_chip, on_chip, pl.BlockSpec(memory_space=pltpu.SMEM)] + [anywhere] * 8,
        out_specs=[anywhere] * 3,
        scratch_shapes=scratch,
        compiler_params=pltpu.CompilerParams(
            collective_id=0, has_side_effects=True, vmem_limit_bytes=62 * 1024 * 1024
        ),
    )(
        dest_offset[0, 0].T, slot_patch[0, 0], rotation,
        increments.reshape(pairs, lat_rows, cells),
        remap_weights.reshape(lat_rows, top * patch, cells),
        basis, inv_metric_diag, inv_metric_cross, thickness, wind_first, wind_second,
    )
    return tuple(
        pl.pallas_call(
            copy_kernel,
            out_shape=[jax.ShapeDtypeStruct(thickness.shape, f32)] * 3,
            in_specs=[anywhere] * 3,
            out_specs=[anywhere] * 3,
            scratch_shapes=[vmem((3,) + thickness.shape, f32), dma((3,)), dma((3,))],
        )(*moved)
    )


def copy_kernel(depth, first, second, out_depth, out_first, out_second, held, in_sem, out_sem):
    pairs = ((depth, out_depth), (first, out_first), (second, out_second))
    incoming = [pltpu.make_async_copy(src, held.at[i], in_sem.at[i]) for i, (src, _) in enumerate(pairs)]
    outgoing = [pltpu.make_async_copy(held.at[i], dst, out_sem.at[i]) for i, (_, dst) in enumerate(pairs)]
    for copy in incoming:
        copy.start()
    for arrived, copy in zip(incoming, outgoing):
        arrived.wait()
        copy.start()
    for copy in outgoing:
        copy.wait()


def solution(mesh):
    tile = P(None, "ty", "tx")
    in_specs = (
        P(None, None, "tx", "ty"),
        P("tx", "ty", None, None, None, None),
        P("tx", "ty", None, None),
        P("tx", "ty", None, None),
        P(),
        tile,
        tile,
        P("ty", "tx"),
        tile,
        tile,
        tile,
    )
    return jax.shard_map(body, mesh=mesh, in_specs=in_specs, out_specs=(tile, tile, tile), check_vma=False)
```
